32 devices in a mesh: fsdp: 2 (over y), ctx: 4 (over x, core), tp: 4 (over z).
Axes of the slice: x: 2, y: 2, z: 4, core: 2. Of those that a mesh axis runs over, the one named last changes fastest.
Arguments:
- tokens: bfloat16 [8, 2048, 1024], P('fsdp', 'ctx'), may hold values from -6 to 6
- segments: int32 [8, 2048], P('fsdp'), may hold values from 0 to 10, as said below
- w_qkv: bfloat16 [3, 1024, 1024], P(None, 'fsdp', 'tp'), may hold values from -0.1875 to 0.1875
- b_qv: bfloat16 [2, 16, 64], P(None, 'tp', 'fsdp'), may hold values from -3 to 3
- w_o: bfloat16 [1024, 1024], P('tp', 'fsdp'), may hold values from -3 to 3
- b_o: bfloat16 [1024], P('fsdp'), may hold values from -3 to 3
- ln1_gain: bfloat16 [1024], P('fsdp'), may hold values from 0.5 to 1.5
- ln1_bias: bfloat16 [1024], P('fsdp'), may hold values from -2 to 2
- w_in: bfloat16 [1024, 4096], P('fsdp', 'tp'), may hold values from -0.1875 to 0.1875
- b_in: bfloat16 [64, 64], P('tp', 'fsdp'), may hold values from -3 to 3
- w_out: bfloat16 [4096, 1024], P('tp', 'fsdp'), may hold values from -0.09375 to 0.09375
- b_out: bfloat16 [1024], P('fsdp'), may hold values from -3 to 3
- ln2_gain: bfloat16 [1024], P('fsdp'), may hold values from 0.5 to 1.5
- ln2_bias: bfloat16 [1024], P('fsdp'), may hold values from -2 to 2
- cotangent: bfloat16 [8, 2048, 1024], P('fsdp', 'ctx'), may hold values from -6 to 6
Outputs:
- output: bfloat16 [8, 2048, 1024], P('fsdp', 'ctx')
- grad_tokens: bfloat16 [8, 2048, 1024], P('fsdp', 'ctx')
- grad_w_qkv: float32 [3, 1024, 1024], P(None, 'fsdp', 'tp')
- grad_b_qv: float32 [2, 16, 64], P(None, 'tp', 'fsdp')
- grad_w_o: float32 [1024, 1024], P('tp', 'fsdp')
- grad_b_o: float32 [1024], P('fsdp')
- grad_ln1_gain: float32 [1024], P('fsdp')
- grad_ln1_bias: float32 [1024], P('fsdp')
- grad_w_in: float32 [1024, 4096], P('fsdp', 'tp')
- grad_b_in: float32 [64, 64], P('tp', 'fsdp')
- grad_w_out: float32 [4096, 1024], P('tp', 'fsdp')
- grad_b_out: float32 [1024], P('fsdp')
- grad_ln2_gain: float32 [1024], P('fsdp')
- grad_ln2_bias: float32 [1024], P('fsdp')
The draws below stay inside these ranges and needn't reach their ends.
Inputs may be any that keep to these rules, and one draw needn't show every extreme that they name: `segments`: in each sequence the ids start at 0 and rise by one at each document boundary; every document has 200 to 2000 tokens except a sequence's last, which ends with the sequence and may be shorter; one document of the batch has exactly 2000 tokens, and one sequence is made of documents of exactly 200 tokens except its last.
All inputs are finite; a program needn't handle non-finite values.
Results may differ from the reference program's by a relative error of at most 0.02.
Values may be sent and summed in bfloat16 or wider, within the bound.
No kernel may reach another device: no remote copies, remote signals or barrier semaphores. Data moves between devices by JAX's collectives and lax.ppermute only.
A program may use at most 192 MiB of HBM per device.

```python
import jax
import jax.numpy as jnp
from jax import lax

D = 1024
HEADS = 16
HD = 64
FF = 4096
LEN = 2048
DOC_MIN = 200
DOC_MAX = 2000
SEQS = 8


def draw_segments(key, part):
    doc_count = LEN // DOC_MIN + 1
    lengths = jax.random.randint(jax.random.fold_in(key, 11), (SEQS, doc_count), DOC_MIN, DOC_MAX + 1)
    chosen = jax.random.randint(jax.random.fold_in(key, 12), (), 0, SEQS)
    shortest = (jnp.arange(SEQS) == (chosen + 1) % SEQS)[:, None]
    lengths = jnp.where(shortest, DOC_MIN, lengths)
    first_doc = (jnp.arange(SEQS) == chosen)[:, None] & (jnp.arange(doc_count) == 0)[None, :]
    lengths = jnp.where(first_doc, DOC_MAX, lengths)
    ends = jnp.cumsum(lengths, axis=1)
    places = jnp.arange(LEN)
    return jnp.sum((ends[:, None, :] <= places[None, :, None]).astype(jnp.int32), axis=2).astype(jnp.int32)


def steps_of(rng, dims, split, low, top_value):
    factor_of = 1.0
    for dim, blocks in split:
        heights = jax.random.uniform(jax.random.fold_in(jax.random.fold_in(rng, 6), dim), (blocks,), jnp.float32, low / len(split), top_value / len(split))
        factor_of = factor_of * jnp.repeat(jnp.exp(heights), dims[dim] // blocks).reshape((-1,) + (1,) * (len(dims) - 1 - dim))
    return factor_of


def scatter_about(own_key, extent, width, bound, pieces=(), dtype=jnp.bfloat16):
    gain = steps_of(own_key, extent, pieces, -0.22, 0.18) if pieces else 1.0
    result = jax.random.normal(own_key, extent, jnp.float32) * width * gain
    return jnp.minimum(jnp.maximum(result, -bound), bound).astype(dtype)


def setup_inputs(seed: int = 0) -> dict:
    seeds = jax.random.split(jax.random.key(seed), 16)
    return {
        "tokens": scatter_about(seeds[0], (SEQS, LEN, D), 1.0, 6.0, ((0, 2), (1, 4))),
        "segments": draw_segments(jax.random.fold_in(seeds[15], 71), 0),
        "w_qkv": scatter_about(seeds[2], (3, D, D), D ** -0.5, 0.1875, ((1, 2), (2, 4))),
        "b_qv": scatter_about(seeds[3], (2, HEADS, HD), 0.5, 3.0, ((1, 4), (2, 2))),
        "w_o": scatter_about(seeds[4], (D, D), (max(D // 256, 1)) ** -0.5, 3.0, ((0, 4), (1, 2))),
        "b_o": scatter_about(seeds[5], (D,), 0.5, 3.0, ((0, 2),)),
        "ln1_gain": jnp.clip(1.0 + 0.1 * jax.random.normal(seeds[6], (D,), jnp.float32), 0.5, 1.5).astype(jnp.bfloat16),
        "ln1_bias": scatter_about(seeds[7], (D,), 0.3, 2.0, ((0, 2),)),
        "w_in": scatter_about(seeds[8], (D, FF), D ** -0.5, 0.1875, ((0, 2), (1, 4))),
        "b_in": scatter_about(seeds[9], (FF // 64, 64), 0.5, 3.0, ((0, 4), (1, 2))),
        "w_out": scatter_about(seeds[10], (FF, D), FF ** -0.5, 0.09375, ((0, 4), (1, 2))),
        "b_out": scatter_about(seeds[11], (D,), 0.5, 3.0, ((0, 2),)),
        "ln2_gain": jnp.clip(1.0 + 0.1 * jax.random.normal(seeds[12], (D,), jnp.float32), 0.5, 1.5).astype(jnp.bfloat16),
        "ln2_bias": scatter_about(seeds[13], (D,), 0.3, 2.0, ((0, 2),)),
        "cotangent": scatter_about(seeds[14], (SEQS, LEN, D), 1.0, 6.0, ((0, 2), (1, 4))),
    }


EPSILON = 1e-12
NEG_LARGE = -1e+30
SCALE_QK = 0.125
HIGHEST = lax.Precision.HIGHEST

@jax.custom_vjp
def low(v):
    return lax.optimization_barrier(v.astype(jnp.bfloat16)).astype(jnp.float32)

@jax.custom_vjp
def low_back(v):
    return v

def low_keep(v):
    return (low(v), None)

def low_pass(kept, grad):
    return (grad,)

def back_keep(v):
    return (v, None)

def back_low(kept, grad):
    return (low(grad),)
low.defvjp(low_keep, low_pass)
low_back.defvjp(back_keep, back_low)

def layer_norm(values, gain_vec, offset):
    center = values - lax.optimization_barrier(jnp.mean(values, -1, keepdims=True))
    spread = lax.optimization_barrier(jnp.mean(center * center, -1, keepdims=True))
    return center * lax.rsqrt(spread + EPSILON) * gain_vec + offset

def gelu_exact(values):
    return 0.5 * values * (1.0 + jax.scipy.special.erf(values * 0.7071067811865476))

def attend_head(query_head, key_head, value_head, same_doc):
    scores = low_back(jnp.dot(query_head, key_head.T, precision=HIGHEST) * SCALE_QK)
    scores = jnp.where(same_doc, scores, NEG_LARGE)
    row_max = lax.optimization_barrier(jnp.max(scores, -1, keepdims=True))
    exp_scores = jnp.exp(scores - row_max)
    attn_probs = exp_scores / lax.optimization_barrier(jnp.sum(exp_scores, -1, keepdims=True))
    return jnp.dot(low(attn_probs), value_head, precision=HIGHEST)

def to_heads(rows):
    return rows.reshape(LEN, HEADS, HD).transpose(1, 0, 2)

def forward(layer_in, segment_row, w_qkv, b_qv, w_o, b_o, ln1_gain, ln1_bias, w_in, b_in, w_out, b_out, ln2_gain, ln2_bias):
    query_rows = low_back(low(jnp.dot(layer_in, w_qkv[0], precision=HIGHEST) + b_qv[0].reshape(-1)))
    key_rows = low_back(low(jnp.dot(layer_in, w_qkv[1], precision=HIGHEST)))
    value_rows = low_back(low(jnp.dot(layer_in, w_qkv[2], precision=HIGHEST) + b_qv[1].reshape(-1)))
    same_doc = segment_row[:, None] == segment_row[None, :]

    def per_head(operands):
        return attend_head(operands[0], operands[1], operands[2], same_doc)
    mixed_heads = lax.map(jax.checkpoint(per_head), (to_heads(query_rows), to_heads(key_rows), to_heads(value_rows)))
    attended = low_back(low(mixed_heads.transpose(1, 0, 2).reshape(LEN, D)))
    attn_rows = low_back(jnp.dot(attended, w_o, precision=HIGHEST) + b_o)
    normed = layer_norm(layer_in + attn_rows, ln1_gain, ln1_bias)
    pre_act = low_back(jnp.dot(low(normed), w_in, precision=HIGHEST) + b_in.reshape(-1))
    act_low = low(gelu_exact(pre_act))
    mlp_rows = low_back(jnp.dot(act_low, w_out, precision=HIGHEST) + b_out)
    return layer_norm(normed + mlp_rows, ln2_gain, ln2_bias)

def reference(tokens, segments, w_qkv, b_qv, w_o, b_o, ln1_gain, ln1_bias, w_in, b_in, w_out, b_out, ln2_gain, ln2_bias, cotangent):
    params = tuple((param_value.astype(jnp.float32) for param_value in (w_qkv, b_qv, w_o, b_o, ln1_gain, ln1_bias, w_in, b_in, w_out, b_out, ln2_gain, ln2_bias)))

    def one_sequence(totals, sequence):
        layer_in, segment_row, grad_out = sequence

        def apply_layer(inputs, *weights):
            return forward(inputs, segment_row, *weights)
        final_rows, pullback = jax.vjp(apply_layer, layer_in.astype(jnp.float32), *params)
        gradients = pullback(grad_out.astype(jnp.float32))
        updated = tuple((earlier + latest for earlier, latest in zip(totals, gradients[1:])))
        return (updated, (final_rows.astype(jnp.bfloat16), gradients[0].astype(jnp.bfloat16)))
    initial = tuple((jnp.zeros_like(param_value) for param_value in params))
    summed, (output, grad_tokens) = lax.scan(one_sequence, initial, (tokens, segments, cotangent))
    return (output, grad_tokens, summed[0], summed[1], summed[2], summed[3], summed[4], summed[5], summed[6], summed[7], summed[8], summed[9], summed[10], summed[11])
```

```python
import functools

import jax
import jax.numpy as jnp
from jax import lax
from jax.experimental import pallas as pl
from jax.experimental.pallas import tpu as pltpu
from jax.sharding import PartitionSpec as P

EPSILON = 1e-12
NEG_LARGE = -1e30
SCALE_QK = 0.125
LOG2_E = 1.4426950408889634
SCALE_LOG2 = SCALE_QK * LOG2_E
LANES = 128
BF16 = jnp.bfloat16
F32 = jnp.float32
CONTRACT_LAST = (((1,), (1,)), ((), ()))
CONTRACT_FIRST = (((0,), (0,)), ((), ()))


def layer_norm(values, gain_vec, offset):
    center = values - jnp.mean(values, -1, keepdims=True)
    spread = jnp.mean(center * center, -1, keepdims=True)
    return center * lax.rsqrt(spread + EPSILON) * gain_vec + offset


def gelu_exact(values):
    return 0.5 * values * (1.0 + lax.erf(values * 0.7071067811865476))


def gelu_slope(values):
    normal_cdf = 0.5 * (1.0 + lax.erf(values * 0.7071067811865476))
    return normal_cdf + values * jnp.exp(-0.5 * values * values) * 0.3989422804014327


def dot_nt(left, right):
    return lax.dot_general(left, right, CONTRACT_LAST, preferred_element_type=F32)


def dot_tn(left, right):
    return lax.dot_general(left, right, CONTRACT_FIRST, preferred_element_type=F32)


def dot_nn(left, right):
    return jnp.dot(left, right, preferred_element_type=F32)


def attend_kernel(head_size, q_ref, k_ref, v_ref, sq_ref, sk_ref, o_ref, lse_ref):
    lane_head = lax.broadcasted_iota(jnp.int32, (1, LANES), 1) // head_size
    query, key, value = q_ref[0], k_ref[0], v_ref[0]
    same_doc = sq_ref[0] == sk_ref[0]
    heads = LANES // head_size
    mixed = jnp.zeros(query.shape, F32)
    lse = jnp.zeros(query.shape, F32)
    for head in range(heads):
        own = lane_head == head
        scores = dot_nt(jnp.where(own, query, jnp.zeros_like(query)), key)
        scores = jnp.where(same_doc, scores, NEG_LARGE)
        row_max = jnp.max(scores, -1, keepdims=True)
        exp_scores = jnp.exp2((scores - row_max) * SCALE_LOG2)
        denominator = jnp.sum(exp_scores, -1, keepdims=True)
        part = dot_nn(exp_scores.astype(BF16), value) / denominator
        mixed = jnp.where(own, part, mixed)
        lse = jnp.where(own, row_max * SCALE_LOG2 + jnp.log2(denominator), lse)
    o_ref[0] = mixed.astype(BF16)
    turned = lse.T
    for head in range(heads):
        lse_ref[0, 0, head : head + 1, :] = turned[head * head_size : head * head_size + 1, :]


def attend(query, key, value, segs, head_size):
    seq_count, length, cols = query.shape
    block = min(256, length)
    pairs = cols // LANES
    flops = 4 * seq_count * length * length * cols
    row_spec = pl.BlockSpec((1, block, LANES), lambda s, p, i: (s, i, p))
    full_spec = pl.BlockSpec((1, length, LANES), lambda s, p, i: (s, 0, p))
    return pl.pallas_call(
        functools.partial(attend_kernel, head_size),
        grid=(seq_count, pairs, length // block),
        in_specs=[
            row_spec,
            full_spec,
            full_spec,
            pl.BlockSpec((1, block, 1), lambda s, p, i: (s, i, 0)),
            pl.BlockSpec((1, 1, length), lambda s, p, i: (s, 0, 0)),
        ],
        out_specs=[row_spec, pl.BlockSpec((1, 1, 8, block), lambda s, p, i: (s, p, 0, i))],
        out_shape=[
            jax.ShapeDtypeStruct(query.shape, BF16),
            jax.ShapeDtypeStruct((seq_count, pairs, 8, length), F32),
        ],
        compiler_params=pltpu.CompilerParams(vmem_limit_bytes=48 << 20),
        cost_estimate=pl.CostEstimate(
            flops=flops,
            bytes_accessed=8 * seq_count * length * cols,
            transcendentals=seq_count * length * length * cols // head_size,
        ),
        name="attend",
    )(query, key, value, segs[:, :, None], segs[:, None, :])


def attend_grad_kernel(
    head_size,
    q_ref,
    do_ref,
    o_ref,
    k_ref,
    v_ref,
    sq_ref,
    sk_ref,
    lse_ref,
    dq_ref,
    dk_ref,
    dv_ref,
    kt_ref,
    dk_sum,
    dv_sum,
):
    step = pl.program_id(2)
    lane_head = lax.broadcasted_iota(jnp.int32, (1, LANES), 1) // head_size
    query, grad_out, key, value = q_ref[0], do_ref[0], k_ref[0], v_ref[0]

    @pl.when(step == 0)
    def _():
        kt_ref[...] = k_ref[0].T
        dk_sum[...] = jnp.zeros_like(dk_sum)
        dv_sum[...] = jnp.zeros_like(dv_sum)

    same_doc = sk_ref[0] == sq_ref[0]
    products = (grad_out.astype(F32) * o_ref[0].astype(F32)).T
    grad_query = []
    for head in range(LANES // head_size):
        own = lane_head == head
        rows = slice(head * head_size, (head + 1) * head_size)
        row_delta = jnp.sum(products[rows], 0, keepdims=True)
        query_own = jnp.where(own, query, jnp.zeros_like(query))
        grad_own = jnp.where(own, grad_out, jnp.zeros_like(grad_out))
        scores = dot_nt(key, query_own) * SCALE_LOG2 - lse_ref[0, 0, head : head + 1, :]
        probs = jnp.exp2(jnp.where(same_doc, scores, NEG_LARGE))
        grad_probs = dot_nt(value, grad_own)
        grad_scores = (probs * (grad_probs - row_delta)).astype(BF16)
        dv_sum[...] += dot_nn(probs.astype(BF16), grad_own)
        dk_sum[...] += dot_nn(grad_scores, query_own)
        grad_query.append(dot_nn(kt_ref[rows, :], grad_scores))
    dq_ref[0] = (jnp.concatenate(grad_query, 0).T * SCALE_QK).astype(BF16)

    @pl.when(step == pl.num_programs(2) - 1)
    def _():
        dk_ref[0] = (dk_sum[...] * SCALE_QK).astype(BF16)
        dv_ref[0] = dv_sum[...].astype(BF16)


def attend_grad(query, grad_out, mixed, key, value, segs, lse, head_size):
    seq_count, length, cols = query.shape
    block = min(256, length)
    pairs = cols // LANES
    row_spec = pl.BlockSpec((1, block, LANES), lambda s, p, i: (s, i, p))
    full_spec = pl.BlockSpec((1, length, LANES), lambda s, p, i: (s, 0, p))
    return pl.pallas_call(
        functools.partial(attend_grad_kernel, head_size),
        grid=(seq_count, pairs, length // block),
        in_specs=[
            row_spec,
            row_spec,
            row_spec,
            full_spec,
            full_spec,
            pl.BlockSpec((1, 1, block), lambda s, p, i: (s, 0, i)),
            pl.BlockSpec((1, length, 1), lambda s, p, i: (s, 0, 0)),
            pl.BlockSpec((1, 1, 8, block), lambda s, p, i: (s, p, 0, i)),
        ],
        out_specs=[row_spec, full_spec, full_spec],
        out_shape=[jax.ShapeDtypeStruct(query.shape, BF16)] * 3,
        scratch_shapes=[
            pltpu.VMEM((LANES, length), BF16),
            pltpu.VMEM((length, LANES), F32),
            pltpu.VMEM((length, LANES), F32),
        ],
        compiler_params=pltpu.CompilerParams(vmem_limit_bytes=56 << 20),
        cost_estimate=pl.CostEstimate(
            flops=10 * seq_count * length * length * cols,
            bytes_accessed=16 * seq_count * length * cols,
            transcendentals=seq_count * length * length * cols // head_size,
        ),
        name="attend_grad",
    )(query, grad_out, mixed, key, value, segs[:, None, :], segs[:, :, None], lse)


def local(
    sizes,
    tokens,
    segments,
    w_qkv,
    b_qv,
    w_o,
    b_o,
    ln1_gain,
    ln1_bias,
    w_in,
    b_in,
    w_out,
    b_out,
    ln2_gain,
    ln2_bias,
    cotangent,
):
    fsdp, ctx, tp = sizes
    at_fsdp, at_ctx, at_tp = (lax.axis_index(a) for a in ("fsdp", "ctx", "tp"))
    fsdp_bits, ctx_bits = fsdp.bit_length() - 1, ctx.bit_length() - 1
    low_ctx = ctx // 2
    seqs, block_len, width = tokens.shape
    own_seqs = seqs // tp
    rows = own_seqs * block_len
    length = segments.shape[1]
    head_size = b_qv.shape[2] * fsdp
    head_cols = w_qkv.shape[2] // ctx
    hidden = w_in.shape[1] // ctx
    width_part = width // fsdp

    def exchange(values, axis, size, j):
        return lax.ppermute(values, axis, [(i, i ^ j) for i in range(size)])

    def shift_tp(values):
        return lax.ppermute(values, "tp", [(i, (i + 1) % tp) for i in range(tp)])

    def reorder(blocks, place, bits, axis):
        size = blocks.shape[axis]
        for bit in range(bits):
            order = [i ^ (1 << bit) for i in range(size)]
            turned = jnp.stack([lax.index_in_dim(blocks, i, axis, False) for i in order], axis)
            blocks = jnp.where((place >> bit) & 1 == 1, turned, blocks)
        return blocks

    def reorder_width(values):
        if fsdp == 1:
            return values
        blocks = values.reshape(values.shape[0], fsdp, width_part)
        for bit in range(fsdp_bits):
            order = [i ^ (1 << bit) for i in range(fsdp)]
            parts = [values[:, i * width_part : (i + 1) * width_part] for i in order]
            values = jnp.where((at_fsdp >> bit) & 1 == 1, jnp.concatenate(parts, 1), values)
        del blocks
        return values

    def tp_pieces(piece):
        pieces = [piece]
        for _ in range(tp - 1):
            piece = shift_tp(piece)
            pieces.append(piece)
        return pieces

    def gather_width(values):
        for bit in range(fsdp_bits):
            values = jnp.concatenate([values, exchange(values, "fsdp", fsdp, 1 << bit)], 1)
        return values

    def rows_at(values, place, count):
        return lax.dynamic_slice_in_dim(values, place * count, count, 0)

    qkv_turned = jnp.swapaxes(w_qkv, 1, 2)
    qkv_piece = lax.dynamic_slice_in_dim(qkv_turned, at_ctx * head_cols, head_cols, 1).reshape(
        3 * head_cols, width_part
    )
    small_width = [v.reshape(1, -1) for v in (b_o, ln1_gain, ln1_bias, b_out, ln2_gain, ln2_bias)]
    small_tail = jnp.concatenate([b_qv.reshape(-1), b_in.reshape(-1)])
    tail_rows = -(-small_tail.shape[0] // width_part)
    small_tail = jnp.pad(small_tail, (0, tail_rows * width_part - small_tail.shape[0]))
    small = jnp.concatenate(small_width + [small_tail.reshape(tail_rows, width_part)], 0)
    small = jnp.pad(small, ((0, -small.shape[0] % 16), (0, 0)))
    small_rows = small.shape[0]
    first_pieces = tp_pieces(jnp.concatenate([qkv_piece, small], 0))
    first_parts = [p[i * head_cols : (i + 1) * head_cols] for i in range(3) for p in first_pieces]
    first_parts += [p[3 * head_cols :] for p in first_pieces]
    first_full = gather_width(jnp.concatenate(first_parts, 0))
    qkv_rows = 3 * tp * head_cols
    small_full = first_full[qkv_rows:].reshape(tp, small_rows, fsdp, width_part)

    def spread_ctx(values, bits):
        blocks = [values]
        for bit in range(bits):
            blocks = blocks + [exchange(b, "ctx", ctx, 1 << bit) for b in blocks]
        return blocks

    qkv_weights = spread_ctx(first_full[:qkv_rows], ctx_bits)
    o_piece = jnp.concatenate(tp_pieces(rows_at(w_o, at_ctx, head_cols)), 0)
    o_weights = jnp.concatenate(spread_ctx(gather_width(o_piece), ctx_bits), 0)
    in_piece = rows_at(w_in.T, at_ctx, hidden)
    in_own = gather_width(jnp.concatenate(tp_pieces(in_piece), 0))
    in_own = jnp.concatenate(spread_ctx(in_own, ctx_bits - 1), 0)
    in_weights = [in_own, exchange(in_own, "ctx", ctx, low_ctx)]
    out_weights = []
    for half in range(2):
        piece = rows_at(w_out, at_ctx ^ (half * low_ctx), hidden)
        piece = gather_width(jnp.concatenate(tp_pieces(piece), 0))
        out_weights.append(jnp.concatenate(spread_ctx(piece, ctx_bits - 1), 0))

    own_small = small_full[0].astype(F32)
    bias_attn, gain_one, shift_one, bias_out, gain_two, shift_two = (
        own_small[i].reshape(1, width) for i in range(6)
    )
    fsdp_order = at_fsdp ^ jnp.arange(fsdp)
    ctx_order = at_ctx ^ jnp.arange(ctx)
    tails = small_full[:, 6 : 6 + tail_rows].astype(F32)
    tails = jnp.take(tails.transpose(2, 0, 1, 3), fsdp_order, axis=0)
    tails = tails.reshape(fsdp, tp, tail_rows * width_part)
    head_count = b_qv.shape[1]
    qv_tail = tails[:, :, : b_qv.size].reshape(fsdp, tp, 2, head_count, head_size // fsdp)
    qv_bias = qv_tail.transpose(2, 1, 3, 0, 4).reshape(2, tp, ctx, head_cols)
    qv_bias = jnp.take(qv_bias, ctx_order, axis=2).transpose(2, 0, 1, 3)
    qv_bias = qv_bias.reshape(ctx, 2, tp * head_cols)
    in_tail = tails[:, :, b_qv.size : b_qv.size + b_in.size]
    in_tail = in_tail.reshape(fsdp, tp, b_in.shape[0], b_in.shape[1])
    in_bias = in_tail.transpose(1, 2, 0, 3).reshape(tp, ctx, hidden)
    in_bias = jnp.take(in_bias, ctx_order, axis=1).transpose(1, 0, 2)
    in_bias = in_bias.reshape(2, 1, low_ctx * tp * hidden)

    def own_rows(values):
        values = lax.dynamic_slice_in_dim(values, at_tp * own_seqs, own_seqs, 0)
        return reorder_width(values.reshape(rows, width))

    inputs, grad_final = own_rows(tokens), own_rows(cotangent)
    own_segments = lax.dynamic_slice_in_dim(segments, at_tp * own_seqs, own_seqs, 0)
    seg_blocks = own_segments.reshape(own_seqs, ctx, block_len)
    segs = jnp.concatenate(
        [
            lax.dynamic_index_in_dim(seg_blocks, at_ctx ^ j, 1, False)
            for j in range(ctx)
        ],
        1,
    )

    split_cols = width // ctx
    aligned = head_cols % head_size == 0
    if not aligned:
        want = ctx_order[:, None] * split_cols + jnp.arange(split_cols)[None, :]
        shard, inner = want // (ctx * head_cols), want % (ctx * head_cols)
        part, offset = inner // head_cols, inner % head_cols
        to_heads = ((part ^ at_ctx) * tp + (at_tp - shard) % tp) * head_cols + offset
        to_heads = to_heads.reshape(-1)
        from_heads = jnp.zeros_like(to_heads).at[to_heads].set(jnp.arange(width))

    def head_blocks(blocks):
        if aligned:
            return blocks
        moved = jnp.take(jnp.concatenate(blocks, 1), to_heads, axis=1)
        return [moved[:, j * split_cols : (j + 1) * split_cols] for j in range(ctx)]

    def column_blocks(blocks):
        if aligned:
            return blocks
        moved = jnp.take(jnp.concatenate(blocks, 1), from_heads, axis=1)
        return [moved[:, j * split_cols : (j + 1) * split_cols] for j in range(ctx)]

    def to_sequences(blocks):
        arrived = [blocks[0]] + [exchange(blocks[j], "ctx", ctx, j) for j in range(1, ctx)]
        cols = blocks[0].shape[1]
        return jnp.concatenate([b.reshape(own_seqs, block_len, cols) for b in arrived], 1)

    def to_rows(values):
        cols = values.shape[2]
        blocks = [
            values[:, j * block_len : (j + 1) * block_len].reshape(rows, cols) for j in range(ctx)
        ]
        return [blocks[0]] + [exchange(blocks[j], "ctx", ctx, j) for j in range(1, ctx)]

    qkv_blocks = []
    zero_bias = jnp.zeros((1, split_cols), F32)
    for j in range(ctx):
        bias = jnp.concatenate([qv_bias[j, 0:1], zero_bias, qv_bias[j, 1:2]], 1)
        qkv_blocks.append((dot_nt(inputs, qkv_weights[j]) + bias).astype(BF16))
    if not aligned:
        parts = [
            head_blocks([b[:, i * split_cols : (i + 1) * split_cols] for b in qkv_blocks])
            for i in range(3)
        ]
        qkv_blocks = [jnp.concatenate([p[j] for p in parts], 1) for j in range(ctx)]
    qkv_seq = to_sequences(qkv_blocks)
    query, key, value = (qkv_seq[:, :, i * split_cols : (i + 1) * split_cols] for i in range(3))
    mixed, lse = attend(query, key, value, segs, head_size)
    attended = jnp.concatenate(column_blocks(to_rows(mixed)), 1)

    attn_rows = dot_nn(attended, o_weights) + bias_attn
    first_in = inputs.astype(F32) + attn_rows
    normed, pull_first = jax.vjp(layer_norm, first_in, gain_one, shift_one)
    normed_low = normed.astype(BF16)
    pre_act = [dot_nt(normed_low, in_weights[h]) + in_bias[h] for h in range(2)]
    act_low = [gelu_exact(p).astype(BF16) for p in pre_act]
    mlp_rows = dot_nn(act_low[0], out_weights[0]) + dot_nn(act_low[1], out_weights[1]) + bias_out
    final_rows, pull_second = jax.vjp(layer_norm, normed + mlp_rows, gain_two, shift_two)

    def share_rows(values):
        values = reorder_width(values.astype(BF16)).reshape(own_seqs, block_len, width)
        pieces = tp_pieces(values)
        whole = jnp.zeros((seqs, block_len, width), BF16)
        for s in range(tp):
            start = ((at_tp - s) % tp) * own_seqs
            whole = lax.dynamic_update_slice_in_dim(whole, pieces[s], start, 0)
        return whole

    output = share_rows(final_rows)

    def add_low(left, right):
        return (left.astype(F32) + right.astype(F32)).astype(BF16)

    def fold_rows(values, bit):
        half = values.shape[0] // 2
        return add_low(values[:half], exchange(values[half:], "ctx", ctx, 1 << bit))

    def fold_width(values):
        for bit in reversed(range(fsdp_bits)):
            half = values.shape[1] // 2
            values = add_low(values[:, :half], exchange(values[:, half:], "fsdp", fsdp, 1 << bit))
        return values

    def fold_tp(pieces):
        total = pieces[1 % tp]
        for s in range(2, tp + 1):
            total = add_low(shift_tp(total), pieces[s % tp])
        return total

    def sum_shares(halves, width_first, split):
        for bit in reversed(range(ctx_bits - 1)):
            halves = [fold_rows(h, bit) for h in halves]
        if width_first:
            halves = [fold_width(h) for h in halves]
        total = add_low(halves[0], exchange(halves[1], "ctx", ctx, low_ctx))
        if not width_first:
            total = fold_width(total)
        return fold_tp(split(total))

    def split_even(total):
        count = total.shape[0] // tp
        return [total[s * count : (s + 1) * count] for s in range(tp)]

    def split_qkv(total):
        cut = [total[i * head_cols : (i + 1) * head_cols] for i in range(3 * tp)]
        return [jnp.concatenate([cut[i * tp + s] for i in range(3)], 0) for s in range(tp)]

    def join_ctx(share):
        blocks = jnp.stack(spread_ctx(share, ctx_bits), 0)
        return reorder(blocks, at_ctx, ctx_bits, 0).astype(F32)

    grad_second, grad_gain_second, grad_shift_second = pull_second(grad_final.astype(F32))
    grad_mlp = grad_second.astype(BF16)
    grad_bias_out = jnp.sum(grad_mlp, 0, dtype=F32)
    grad_pre, grad_out_halves, grad_in_halves = [], [], []
    for h in range(2):
        grad_out_halves.append(dot_tn(act_low[h], grad_mlp).astype(BF16))
    share_out = sum_shares(grad_out_halves, False, split_even)
    for h in range(2):
        grad_pre.append((dot_nt(grad_mlp, out_weights[h]) * gelu_slope(pre_act[h])).astype(BF16))
    grad_bias_in = jnp.stack([jnp.sum(g, 0, dtype=F32) for g in grad_pre])
    grad_normed = grad_second + (dot_nn(grad_pre[0], in_weights[0]) + dot_nn(grad_pre[1], in_weights[1]))
    grad_first, grad_gain_first, grad_shift_first = pull_first(grad_normed)
    grad_attn = grad_first.astype(BF16)
    grad_bias_attn = jnp.sum(grad_attn, 0, dtype=F32)
    grad_attended = dot_nt(grad_attn, o_weights).astype(BF16)
    grad_blocks = head_blocks(
        [grad_attended[:, j * split_cols : (j + 1) * split_cols] for j in range(ctx)]
    )
    grad_mixed = to_sequences(grad_blocks)
    for h in range(2):
        grad_in_halves.append(dot_tn(grad_pre[h], normed_low).astype(BF16))
    share_in = sum_shares(grad_in_halves, True, split_even)
    grad_o = dot_tn(attended, grad_attn).astype(BF16)
    half_o = grad_o.shape[0] // 2
    share_o = sum_shares([grad_o[:half_o], grad_o[half_o:]], True, split_even)

    grad_seq = jnp.concatenate(
        attend_grad(query, grad_mixed, mixed, key, value, segs, lse, head_size), 2
    )
    grad_qkv = to_rows(grad_seq)
    if not aligned:
        parts = [
            column_blocks([b[:, i * split_cols : (i + 1) * split_cols] for b in grad_qkv])
            for i in range(3)
        ]
        grad_qkv = [jnp.concatenate([p[j] for p in parts], 1) for j in range(ctx)]
    input_part = dot_nn(grad_qkv[0], qkv_weights[0])
    for j in range(1, ctx):
        input_part = input_part + dot_nn(grad_qkv[j], qkv_weights[j])
    grad_tokens = share_rows(grad_first + input_part)
    grad_qkv_w = [dot_tn(g, inputs).astype(BF16) for g in grad_qkv]

    def sum_qkv(blocks):
        total = [
            add_low(blocks[j], exchange(blocks[j + low_ctx], "ctx", ctx, low_ctx))
            for j in range(low_ctx)
        ]
        for bit in reversed(range(ctx_bits - 1)):
            half = len(total) // 2
            total = [
                add_low(total[j], exchange(total[j + half], "ctx", ctx, 1 << bit))
                for j in range(half)
            ]
        return fold_tp(split_qkv(fold_width(total[0])))

    share_qkv = sum_qkv(grad_qkv_w)

    def ctx_tp_order(values):
        blocks = values.reshape(values.shape[0], ctx, tp, -1)
        blocks = jnp.take(blocks, ctx_order, axis=1)
        blocks = jnp.take(blocks, (at_tp - jnp.arange(tp)) % tp, axis=2)
        return blocks.transpose(0, 2, 1, 3).reshape(values.shape[0], -1)

    def total_sum(values):
        for axis, size in (("ctx", ctx), ("fsdp", fsdp), ("tp", tp)):
            for bit in range(size.bit_length() - 1):
                values = values + exchange(values, axis, size, 1 << bit)
        return values

    small_sums = jnp.stack(
        [
            v.reshape(-1)
            for v in (
                grad_bias_attn,
                grad_gain_first,
                grad_shift_first,
                grad_bias_out,
                grad_gain_second,
                grad_shift_second,
            )
        ]
    )
    hidden_sums = ctx_tp_order(grad_bias_in.reshape(1, -1)).reshape(-1, width)
    small_sums = jnp.concatenate([reorder_width(small_sums), hidden_sums], 0)
    small_sums = total_sum(small_sums)
    width_start = at_fsdp * width_part
    width_sums = lax.dynamic_slice_in_dim(small_sums[:6], width_start, width_part, 1)
    hidden_own = lax.dynamic_slice_in_dim(
        small_sums[6:].reshape(tp, b_in.shape[0], fsdp, b_in.shape[1]), at_tp, 1, 0
    )
    grad_b_in = lax.dynamic_index_in_dim(hidden_own[0], at_fsdp, 1, False)
    qv_sums = [
        jnp.stack(
            [
                jnp.sum(g[:, i * split_cols : (i + 1) * split_cols], 0, dtype=F32)
                for g in grad_qkv
            ]
        )
        for i in (0, 2)
    ]
    qv_sums = total_sum(ctx_tp_order(jnp.stack(qv_sums).reshape(2, -1)))
    qv_own = lax.dynamic_index_in_dim(
        qv_sums.reshape(2, tp, head_count, fsdp, head_size // fsdp), at_tp, 1, False
    )
    grad_b_qv = lax.dynamic_index_in_dim(qv_own, at_fsdp, 2, False)

    grad_w_qkv = join_ctx(share_qkv.reshape(3, head_cols, width_part))
    grad_w_qkv = grad_w_qkv.transpose(1, 3, 0, 2).reshape(3, width_part, ctx * head_cols)
    grad_w_o = join_ctx(share_o).reshape(ctx * head_cols, width_part)
    grad_w_in = join_ctx(share_in).reshape(ctx * hidden, width_part).T
    grad_w_out = join_ctx(share_out).reshape(ctx * hidden, width_part)
    return (
        output,
        grad_tokens,
        grad_w_qkv,
        grad_b_qv,
        grad_w_o,
        width_sums[0],
        width_sums[1],
        width_sums[2],
        grad_w_in,
        grad_b_in,
        grad_w_out,
        width_sums[3],
        width_sums[4],
        width_sums[5],
    )


def solution(mesh):
    in_specs = (
        P("fsdp", "ctx", None),
        P("fsdp", None),
        P(None, "fsdp", "tp"),
        P(None, "tp", "fsdp"),
        P("tp", "fsdp"),
        P("fsdp"),
        P("fsdp"),
        P("fsdp"),
        P("fsdp", "tp"),
        P("tp", "fsdp"),
        P("tp", "fsdp"),
        P("fsdp"),
        P("fsdp"),
        P("fsdp"),
        P("fsdp", "ctx", None),
    )
    out_specs = (
        P("fsdp", "ctx", None),
        P("fsdp", "ctx", None),
        P(None, "fsdp", "tp"),
        P(None, "tp", "fsdp"),
        P("tp", "fsdp"),
        P("fsdp"),
        P("fsdp"),
        P("fsdp"),
        P("fsdp", "tp"),
        P("tp", "fsdp"),
        P("tp", "fsdp"),
        P("fsdp"),
        P("fsdp"),
        P("fsdp"),
    )
    sizes = tuple(mesh.shape[a] for a in ("fsdp", "ctx", "tp"))
    body = functools.partial(local, sizes)
    return jax.shard_map(body, mesh=mesh, in_specs=in_specs, out_specs=out_specs, check_vma=False)
```

```python
import functools

import jax
import jax.numpy as jnp
from jax import lax
from jax.experimental import pallas as pl
from jax.experimental.pallas import tpu as pltpu
from jax.sharding import PartitionSpec as P

EPSILON = 1e-12
NEG_LARGE = -1e30
SCALE_QK = 0.125
LOG2_E = 1.4426950408889634
SCALE_LOG2 = SCALE_QK * LOG2_E
LANES = 128
BF16 = jnp.bfloat16
F32 = jnp.float32
CONTRACT_LAST = (((1,), (1,)), ((), ()))
CONTRACT_FIRST = (((0,), (0,)), ((), ()))


def layer_norm(values, gain_vec, offset):
    center = values - jnp.mean(values, -1, keepdims=True)
    spread = jnp.mean(center * center, -1, keepdims=True)
    return center * lax.rsqrt(spread + EPSILON) * gain_vec + offset


def gelu_exact(values):
    return 0.5 * values * (1.0 + lax.erf(values * 0.7071067811865476))


def gelu_slope(values):
    normal_cdf = 0.5 * (1.0 + lax.erf(values * 0.7071067811865476))
    return normal_cdf + values * jnp.exp(-0.5 * values * values) * 0.3989422804014327


def dot_nt(left, right):
    return lax.dot_general(left, right, CONTRACT_LAST, preferred_element_type=F32)


def dot_tn(left, right):
    return lax.dot_general(left, right, CONTRACT_FIRST, preferred_element_type=F32)


def dot_nn(left, right):
    return jnp.dot(left, right, preferred_element_type=F32)


def attend_kernel(head_size, q_ref, k_ref, v_ref, sq_ref, sk_ref, o_ref, lse_ref):
    lane_head = lax.broadcasted_iota(jnp.int32, (1, LANES), 1) // head_size
    query, key, value = q_ref[0], k_ref[0], v_ref[0]
    same_doc = sq_ref[0] == sk_ref[0]
    heads = LANES // head_size
    mixed = jnp.zeros(query.shape, F32)
    lse = jnp.zeros(query.shape, F32)
    for head in range(heads):
        own = lane_head == head
        scores = dot_nt(jnp.where(own, query, jnp.zeros_like(query)), key)
        scores = jnp.where(same_doc, scores, NEG_LARGE)
        row_max = jnp.max(scores, -1, keepdims=True)
        exp_scores = jnp.exp2((scores - row_max) * SCALE_LOG2)
        denominator = jnp.sum(exp_scores, -1, keepdims=True)
        part = dot_nn(exp_scores.astype(BF16), value) / denominator
        mixed = jnp.where(own, part, mixed)
        lse = jnp.where(own, row_max * SCALE_LOG2 + jnp.log2(denominator), lse)
    o_ref[0] = mixed.astype(BF16)
    turned = lse.T
    for head in range(heads):
        lse_ref[0, 0, head : head + 1, :] = turned[head * head_size : head * head_size + 1, :]


def attend(query, key, value, segs, head_size):
    seq_count, length, cols = query.shape
    block = min(256, length)
    pairs = cols // LANES
    flops = 4 * seq_count * length * length * cols
    row_spec = pl.BlockSpec((1, block, LANES), lambda s, p, i: (s, i, p))
    full_spec = pl.BlockSpec((1, length, LANES), lambda s, p, i: (s, 0, p))
    return pl.pallas_call(
        functools.partial(attend_kernel, head_size),
        grid=(seq_count, pairs, length // block),
        in_specs=[
            row_spec,
            full_spec,
            full_spec,
            pl.BlockSpec((1, block, 1), lambda s, p, i: (s, i, 0)),
            pl.BlockSpec((1, 1, length), lambda s, p, i: (s, 0, 0)),
        ],
        out_specs=[row_spec, pl.BlockSpec((1, 1, 8, block), lambda s, p, i: (s, p, 0, i))],
        out_shape=[
            jax.ShapeDtypeStruct(query.shape, BF16),
            jax.ShapeDtypeStruct((seq_count, pairs, 8, length), F32),
        ],
        compiler_params=pltpu.CompilerParams(vmem_limit_bytes=48 << 20),
        cost_estimate=pl.CostEstimate(
            flops=flops,
            bytes_accessed=8 * seq_count * length * cols,
            transcendentals=seq_count * length * length * cols // head_size,
        ),
        name="attend",
    )(query, key, value, segs[:, :, None], segs[:, None, :])


def attend_grad_kernel(
    head_size,
    q_ref,
    do_ref,
    o_ref,
    k_ref,
    v_ref,
    sq_ref,
    sk_ref,
    lse_ref,
    dq_ref,
    dk_ref,
    dv_ref,
    kt_ref,
    dk_sum,
    dv_sum,
):
    step = pl.program_id(2)
    lane_head = lax.broadcasted_iota(jnp.int32, (1, LANES), 1) // head_size
    query, grad_out, key, value = q_ref[0], do_ref[0], k_ref[0], v_ref[0]

    @pl.when(step == 0)
    def _():
        kt_ref[...] = k_ref[0].T
        dk_sum[...] = jnp.zeros_like(dk_sum)
        dv_sum[...] = jnp.zeros_like(dv_sum)

    same_doc = sk_ref[0] == sq_ref[0]
    products = (grad_out.astype(F32) * o_ref[0].astype(F32)).T
    grad_query = []
    for head in range(LANES // head_size):
        own = lane_head == head
        rows = slice(head * head_size, (head + 1) * head_size)
        row_delta = jnp.sum(products[rows], 0, keepdims=True)
        query_own = jnp.where(own, query, jnp.zeros_like(query))
        grad_own = jnp.where(own, grad_out, jnp.zeros_like(grad_out))
        scores = dot_nt(key, query_own) * SCALE_LOG2 - lse_ref[0, 0, head : head + 1, :]
        probs = jnp.exp2(jnp.where(same_doc, scores, NEG_LARGE))
        grad_probs = dot_nt(value, grad_own)
        grad_scores = (probs * (grad_probs - row_delta)).astype(BF16)
        dv_sum[...] += dot_nn(probs.astype(BF16), grad_own)
        dk_sum[...] += dot_nn(grad_scores, query_own)
        grad_query.append(dot_nn(kt_ref[rows, :], grad_scores))
    dq_ref[0] = (jnp.concatenate(grad_query, 0).T * SCALE_QK).astype(BF16)

    @pl.when(step == pl.num_programs(2) - 1)
    def _():
        dk_ref[0] = (dk_sum[...] * SCALE_QK).astype(BF16)
        dv_ref[0] = dv_sum[...].astype(BF16)


def attend_grad(query, grad_out, mixed, key, value, segs, lse, head_size):
    seq_count, length, cols = query.shape
    block = min(256, length)
    pairs = cols // LANES
    row_spec = pl.BlockSpec((1, block, LANES), lambda s, p, i: (s, i, p))
    full_spec = pl.BlockSpec((1, length, LANES), lambda s, p, i: (s, 0, p))
    return pl.pallas_call(
        functools.partial(attend_grad_kernel, head_size),
        grid=(seq_count, pairs, length // block),
        in_specs=[
            row_spec,
            row_spec,
            row_spec,
            full_spec,
            full_spec,
            pl.BlockSpec((1, 1, block), lambda s, p, i: (s, 0, i)),
            pl.BlockSpec((1, length, 1), lambda s, p, i: (s, 0, 0)),
            pl.BlockSpec((1, 1, 8, block), lambda s, p, i: (s, p, 0, i)),
        ],
        out_specs=[row_spec, full_spec, full_spec],
        out_shape=[jax.ShapeDtypeStruct(query.shape, BF16)] * 3,
        scratch_shapes=[
            pltpu.VMEM((LANES, length), BF16),
            pltpu.VMEM((length, LANES), F32),
            pltpu.VMEM((length, LANES), F32),
        ],
        compiler_params=pltpu.CompilerParams(vmem_limit_bytes=56 << 20),
        cost_estimate=pl.CostEstimate(
            flops=10 * seq_count * length * length * cols,
            bytes_accessed=16 * seq_count * length * cols,
            transcendentals=seq_count * length * length * cols // head_size,
        ),
        name="attend_grad",
    )(query, grad_out, mixed, key, value, segs[:, None, :], segs[:, :, None], lse)


def local(
    sizes,
    tokens,
    segments,
    w_qkv,
    b_qv,
    w_o,
    b_o,
    ln1_gain,
    ln1_bias,
    w_in,
    b_in,
    w_out,
    b_out,
    ln2_gain,
    ln2_bias,
    cotangent,
):
    fsdp, ctx, tp = sizes
    at_fsdp, at_ctx, at_tp = (lax.axis_index(a) for a in ("fsdp", "ctx", "tp"))
    fsdp_bits, ctx_bits = fsdp.bit_length() - 1, ctx.bit_length() - 1
    low_ctx = ctx // 2
    seqs, block_len, width = tokens.shape
    own_seqs = seqs // tp
    rows = own_seqs * block_len
    length = segments.shape[1]
    head_size = b_qv.shape[2] * fsdp
    head_cols = w_qkv.shape[2] // ctx
    hidden = w_in.shape[1] // ctx
    width_part = width // fsdp

    def exchange(values, axis, size, j):
        return lax.ppermute(values, axis, [(i, i ^ j) for i in range(size)])

    def shift_tp(values):
        return lax.ppermute(values, "tp", [(i, (i + 1) % tp) for i in range(tp)])

    def reorder(blocks, place, bits, axis):
        size = blocks.shape[axis]
        for bit in range(bits):
            order = [i ^ (1 << bit) for i in range(size)]
            turned = jnp.stack([lax.index_in_dim(blocks, i, axis, False) for i in order], axis)
            blocks = jnp.where((place >> bit) & 1 == 1, turned, blocks)
        return blocks

    def reorder_width(values):
        for bit in range(fsdp_bits):
            order = [i ^ (1 << bit) for i in range(fsdp)]
            parts = [values[:, i * width_part : (i + 1) * width_part] for i in order]
            values = jnp.where((at_fsdp >> bit) & 1 == 1, jnp.concatenate(parts, 1), values)
        return values

    def tp_pieces(piece):
        pieces = [piece]
        for _ in range(tp - 1):
            piece = shift_tp(piece)
            pieces.append(piece)
        return pieces

    def gather_width(values):
        for bit in range(fsdp_bits):
            values = jnp.concatenate([values, exchange(values, "fsdp", fsdp, 1 << bit)], 1)
        return values

    def spread_near(values):
        blocks = [values]
        for bit in range(ctx_bits - 1):
            blocks = blocks + [exchange(b, "ctx", ctx, 1 << bit) for b in blocks]
        return blocks

    def near_rows(values, count, both):
        halves = range(2) if both else range(1)
        return [
            lax.dynamic_slice_in_dim(values, (at_ctx ^ (h * low_ctx)) * count, count, 0)
            for h in halves
        ]

    def cut(values, count):
        return [values[i : i + count] for i in range(0, values.shape[0], count)]

    per_group = max(1, LANES // head_cols)
    groups = tp // per_group
    group_cols = per_group * head_cols
    qkv_turned = jnp.swapaxes(w_qkv, 1, 2)
    qkv_pieces = []
    for h in range(2):
        start = (at_ctx ^ (h * low_ctx)) * head_cols
        qkv_pieces.append(
            lax.dynamic_slice_in_dim(qkv_turned, start, head_cols, 1).reshape(
                3 * head_cols, width_part
            )
        )
    small_width = [v.reshape(1, -1) for v in (b_o, ln1_gain, ln1_bias, b_out, ln2_gain, ln2_bias)]
    small_tail = jnp.concatenate([b_qv.reshape(-1), b_in.reshape(-1)])
    tail_rows = -(-small_tail.shape[0] // width_part)
    small_tail = jnp.pad(small_tail, (0, tail_rows * width_part - small_tail.shape[0]))
    small = jnp.concatenate(small_width + [small_tail.reshape(tail_rows, width_part)], 0)
    small = jnp.pad(small, ((0, -small.shape[0] % 16), (0, 0)))
    small_rows = small.shape[0]
    first_rows = 6 * head_cols + small_rows
    with jax.named_scope("get_qkv"):
        first_pieces = tp_pieces(jnp.concatenate(qkv_pieces + [small], 0))
        early = (tp + 1) // 2
        first_full = [
            part
            for group in (first_pieces[:early], first_pieces[early:])
            if group
            for part in cut(gather_width(jnp.concatenate(group, 0)), first_rows)
        ]
        unit = [cut(p[: 6 * head_cols], head_cols) for p in first_full]
        own_qkv = jnp.concatenate(
            [
                unit[g * per_group + s][h * 3 + i]
                for h in range(2)
                for g in range(groups)
                for i in range(3)
                for s in range(per_group)
            ],
            0,
        )
        qkv_weights = spread_near(own_qkv)
    small_full = jnp.stack([p[6 * head_cols :] for p in first_full])
    small_full = small_full.reshape(tp, small_rows, fsdp, width_part)
    with jax.named_scope("get_in"):
        in_piece = near_rows(w_in.T, hidden, False)[0]
        in_own = gather_width(jnp.concatenate(tp_pieces(in_piece), 0))
        in_own = jnp.concatenate([in_own, exchange(in_own, "ctx", ctx, low_ctx)], 0)
        in_weights = spread_near(in_own)
    with jax.named_scope("get_out"):
        o_parts, out_parts = near_rows(w_o, head_cols, True), near_rows(w_out, hidden, True)
        pieces = tp_pieces(jnp.concatenate(o_parts + out_parts, 0))
        o_parts = [p[h * head_cols : (h + 1) * head_cols] for h in range(2) for p in pieces]
        out_parts = [
            p[2 * head_cols + h * hidden : 2 * head_cols + (h + 1) * hidden]
            for h in range(2)
            for p in pieces
        ]
        both_own = gather_width(jnp.concatenate(o_parts + out_parts, 0))
        both_weights = spread_near(both_own)
        o_rows = 2 * tp * head_cols
        o_weights = [w[:o_rows] for w in both_weights]
        out_weights = [w[o_rows:] for w in both_weights]

    own_small = small_full[0].astype(F32)
    bias_attn, gain_one, shift_one, bias_out, gain_two, shift_two = (
        own_small[i].reshape(1, width) for i in range(6)
    )
    fsdp_order = at_fsdp ^ jnp.arange(fsdp)
    ctx_order = at_ctx ^ jnp.arange(ctx)
    tails = small_full[:, 6 : 6 + tail_rows].astype(F32)
    tails = reorder(tails.transpose(2, 0, 1, 3), at_fsdp, fsdp_bits, 0)
    tails = tails.reshape(fsdp, tp, tail_rows * width_part)
    head_count = b_qv.shape[1]
    qv_tail = tails[:, :, : b_qv.size].reshape(fsdp, tp, 2, head_count, head_size // fsdp)
    qv_bias = qv_tail.transpose(2, 1, 3, 0, 4).reshape(2, tp, ctx, head_cols)
    qv_bias = reorder(qv_bias, at_ctx, ctx_bits, 2)
    in_tail = tails[:, :, b_qv.size : b_qv.size + b_in.size]
    in_tail = in_tail.reshape(fsdp, tp, b_in.shape[0], b_in.shape[1])
    in_bias = in_tail.transpose(1, 2, 0, 3).reshape(tp, ctx, hidden)
    in_bias = reorder(in_bias, at_ctx, ctx_bits, 1).reshape(tp, 2, low_ctx, hidden)
    in_bias = in_bias.transpose(2, 1, 0, 3).reshape(low_ctx, 1, 2 * tp * hidden)
    qv_bias = qv_bias.reshape(2, groups, per_group, 2, low_ctx, head_cols)
    qv_bias = qv_bias.transpose(4, 3, 1, 0, 2, 5).reshape(low_ctx, 2, groups, 2, group_cols)
    qkv_bias = jnp.stack([qv_bias[:, :, :, 0], jnp.zeros_like(qv_bias[:, :, :, 0]), qv_bias[:, :, :, 1]], 3)
    qkv_bias = qkv_bias.reshape(low_ctx, 1, 6 * tp * head_cols)

    def own_rows(values):
        values = lax.dynamic_slice_in_dim(values, at_tp * own_seqs, own_seqs, 0)
        return reorder_width(values.reshape(rows, width))

    inputs, grad_final = own_rows(tokens), own_rows(cotangent)
    own_segments = lax.dynamic_slice_in_dim(segments, at_tp * own_seqs, own_seqs, 0)
    seg_blocks = own_segments.reshape(own_seqs, ctx, block_len)
    segs = jnp.concatenate(
        [lax.dynamic_index_in_dim(seg_blocks, at_ctx ^ j, 1, False) for j in range(ctx)], 1
    )

    aligned = head_cols % head_size == 0
    split_cols = width // ctx
    if not aligned:
        want = ctx_order[:, None] * split_cols + jnp.arange(split_cols)[None, :]
        shard, inner = want // (ctx * head_cols), want % (ctx * head_cols)
        part, offset = inner // head_cols, inner % head_cols
        to_heads = ((part ^ at_ctx) * tp + (at_tp - shard) % tp) * head_cols + offset
        to_heads = to_heads.reshape(-1)
        from_heads = jnp.zeros_like(to_heads).at[to_heads].set(jnp.arange(width))

    def move_columns(blocks, order):
        if aligned:
            return blocks
        parts = blocks[0][0].shape[1] // group_cols
        moved = []
        for i in range(parts):
            cols = slice(i * group_cols, (i + 1) * group_cols)
            flat = jnp.concatenate([b[:, cols] for per in blocks for b in per], 1)
            moved.append(jnp.take(flat, order, axis=1))
        result = []
        for j in range(ctx):
            result.append([])
            for g in range(groups):
                start = j * split_cols + g * group_cols
                result[j].append(
                    jnp.concatenate([m[:, start : start + group_cols] for m in moved], 1)
                )
        return result

    def to_sequences(blocks):
        arrived = [blocks[0]] + [exchange(blocks[j], "ctx", ctx, j) for j in range(1, ctx)]
        cols = blocks[0].shape[1]
        return jnp.concatenate([b.reshape(own_seqs, block_len, cols) for b in arrived], 1)

    def to_rows(values):
        cols = values.shape[2]
        blocks = [
            values[:, j * block_len : (j + 1) * block_len].reshape(rows, cols) for j in range(ctx)
        ]
        return [blocks[0]] + [exchange(blocks[j], "ctx", ctx, j) for j in range(1, ctx)]

    def by_block(near_values, cols):
        return [
            [
                near_values[j % low_ctx][
                    :, ((j // low_ctx) * groups + g) * cols : ((j // low_ctx) * groups + g + 1) * cols
                ]
                for g in range(groups)
            ]
            for j in range(ctx)
        ]

    def by_near(blocks):
        return [
            jnp.concatenate(
                [blocks[h * low_ctx + n][g] for h in range(2) for g in range(groups)], 1
            )
            for n in range(low_ctx)
        ]

    qkv_near = [
        (dot_nt(inputs, qkv_weights[n]) + qkv_bias[n]).astype(BF16) for n in range(low_ctx)
    ]
    qkv_blocks = move_columns(by_block(qkv_near, 3 * group_cols), None if aligned else to_heads)
    heads_in, mixed_parts, mixed_blocks = [], [], [[] for _ in range(ctx)]
    for g in range(groups):
        with jax.named_scope("to_sequences"):
            qkv_seq = to_sequences([b[g] for b in qkv_blocks])
        parts = [qkv_seq[:, :, i * group_cols : (i + 1) * group_cols] for i in range(3)]
        mixed, lse = attend(*parts, segs, head_size)
        heads_in.append((parts, lse))
        mixed_parts.append(mixed)
        with jax.named_scope("to_rows"):
            for j, block in enumerate(to_rows(mixed)):
                mixed_blocks[j].append(block)
    attended = by_near(move_columns(mixed_blocks, None if aligned else from_heads))

    attn_rows = bias_attn
    for n in range(low_ctx):
        attn_rows = attn_rows + dot_nn(attended[n], o_weights[n])
    first_in = inputs.astype(F32) + attn_rows
    normed, pull_first = jax.vjp(layer_norm, first_in, gain_one, shift_one)
    normed_low = normed.astype(BF16)
    pre_act = [dot_nt(normed_low, in_weights[n]) + in_bias[n] for n in range(low_ctx)]
    act_low = [gelu_exact(p).astype(BF16) for p in pre_act]
    mlp_rows = bias_out
    for n in range(low_ctx):
        mlp_rows = mlp_rows + dot_nn(act_low[n], out_weights[n])
    final_rows, pull_second = jax.vjp(layer_norm, normed + mlp_rows, gain_two, shift_two)

    def turned_rows(values):
        return reorder_width(values.astype(BF16)).reshape(own_seqs, block_len, width)

    def place_rows(pieces):
        whole = jnp.zeros((seqs, block_len, width), BF16)
        for s in range(tp):
            start = ((at_tp - s) % tp) * own_seqs
            whole = lax.dynamic_update_slice_in_dim(whole, pieces[s], start, 0)
        return whole

    def gate(values, waited):
        values, waited = lax.optimization_barrier((values, waited))
        return values, waited

    output_pieces = [turned_rows(final_rows)]

    def next_output():
        with jax.named_scope("share_output"):
            return shift_tp(output_pieces[-1]) if len(output_pieces) < tp else output_pieces[0]

    def keep_output(piece):
        if len(output_pieces) < tp:
            output_pieces.append(piece)

    def add_low(left, right):
        return (left.astype(F32) + right.astype(F32)).astype(BF16)

    def fold_width(values):
        for bit in reversed(range(fsdp_bits)):
            half = values.shape[1] // 2
            values = add_low(values[:, :half], exchange(values[:, half:], "fsdp", fsdp, 1 << bit))
        return values

    def fold_half(values):
        half = values.shape[0] // 2
        return add_low(values[:half], exchange(values[half:], "ctx", ctx, low_ctx))

    def fold_tp(pieces):
        total = pieces[0].astype(F32)
        for s in range(1, tp):
            pairs = [(t, (t - s) % tp) for t in range(tp)]
            total = total + lax.ppermute(pieces[s], "tp", pairs).astype(F32)
        return total.astype(BF16)

    def fold_near(near_values):
        for bit in reversed(range(ctx_bits - 1)):
            half = len(near_values) // 2
            near_values = [
                add_low(near_values[n], exchange(near_values[n + half], "ctx", ctx, 1 << bit))
                for n in range(half)
            ]
        return near_values[0]

    def join_halves(arrays):
        if len(arrays) == 1:
            return arrays[0]
        tops = [a[: a.shape[0] // 2] for a in arrays]
        return jnp.concatenate(tops + [a[a.shape[0] // 2 :] for a in arrays], 0)

    def join_ctx(share):
        blocks = share
        for bit in range(ctx_bits):
            blocks = jnp.concatenate([blocks, exchange(blocks, "ctx", ctx, 1 << bit)], 0)
        blocks = blocks.reshape((ctx,) + share.shape)
        return reorder(blocks, at_ctx, ctx_bits, 0).astype(F32)

    grad_second, grad_gain_second, grad_shift_second = pull_second(grad_final.astype(F32))
    grad_mlp = grad_second.astype(BF16)
    grad_bias_out = jnp.sum(grad_mlp, 0, dtype=F32)
    with jax.named_scope("sum_out"):
        sum_out = fold_near([dot_tn(a, grad_mlp).astype(BF16) for a in act_low])
    grad_pre = [
        (dot_nt(grad_mlp, out_weights[n]) * gelu_slope(pre_act[n])).astype(BF16)
        for n in range(low_ctx)
    ]
    grad_pre, (sum_out, piece) = gate(grad_pre, (sum_out, next_output()))
    keep_output(piece)
    with jax.named_scope("sum_out"):
        sum_out = fold_width(sum_out)
    grad_bias_in = jnp.stack([jnp.sum(g, 0, dtype=F32) for g in grad_pre])
    with jax.named_scope("sum_in"):
        grad_in = [dot_tn(g, normed_low).astype(BF16) for g in grad_pre]
    grad_normed = grad_second
    for n in range(low_ctx):
        grad_normed = grad_normed + dot_nn(grad_pre[n], in_weights[n])
    grad_first, grad_gain_first, grad_shift_first = pull_first(grad_normed)
    grad_attn = grad_first.astype(BF16)
    grad_bias_attn = jnp.sum(grad_attn, 0, dtype=F32)
    grad_attended = [dot_nt(grad_attn, o_weights[n]).astype(BF16) for n in range(low_ctx)]
    grad_blocks = move_columns(by_block(grad_attended, group_cols), None if aligned else to_heads)
    with jax.named_scope("to_sequences_grad"):
        grad_mixed = to_sequences([jnp.concatenate(b, 1) for b in grad_blocks])
    with jax.named_scope("sum_in"):
        grad_o = [dot_tn(a, grad_attn).astype(BF16) for a in attended]
        sum_in = fold_near([join_halves([i, o]) for i, o in zip(grad_in, grad_o)])
    grad_mixed, (sum_out, sum_in, piece) = gate(grad_mixed, (sum_out, sum_in, next_output()))
    keep_output(piece)
    with jax.named_scope("sum_in"):
        sum_in = fold_width(sum_in)
    with jax.named_scope("sum_out"):
        sum_out = fold_half(sum_out)

    grad_qkv = [[] for _ in range(ctx)]
    for g in range(groups):
        parts, lse = heads_in[g]
        if g == groups - 1:
            parts, (sum_out, piece) = gate(parts, (sum_out, next_output()))
            keep_output(piece)
            with jax.named_scope("sum_out"):
                share_out = fold_tp(cut(sum_out, hidden))
        cols = slice(g * group_cols, (g + 1) * group_cols)
        grads = attend_grad(
            parts[0], grad_mixed[:, :, cols], mixed_parts[g], parts[1], parts[2], segs, lse, head_size
        )
        with jax.named_scope("to_rows_grad"):
            for j, block in enumerate(to_rows(jnp.concatenate(grads, 2))):
                grad_qkv[j].append(block)
    while len(output_pieces) < tp:
        output_pieces.append(next_output())
    output = place_rows(output_pieces)
    grad_qkv, (share_out, sum_in) = gate(grad_qkv, (share_out, sum_in))
    with jax.named_scope("sum_in"):
        sum_in = fold_half(sum_in)
        in_rows = tp * hidden
        in_cut, o_cut = cut(sum_in[:in_rows], hidden), cut(sum_in[in_rows:], head_cols)
        share_in = fold_tp([jnp.concatenate([i, o], 0) for i, o in zip(in_cut, o_cut)])
    with jax.named_scope("join_out_in"):
        joined = join_ctx(jnp.concatenate([share_out, share_in], 0))
        grad_w_out = joined[:, :hidden].reshape(ctx * hidden, width_part)
        grad_w_in = joined[:, hidden : 2 * hidden].reshape(ctx * hidden, width_part).T
        grad_w_o = joined[:, 2 * hidden :].reshape(ctx * head_cols, width_part)
    grad_near = by_near(move_columns(grad_qkv, None if aligned else from_heads))
    input_part = grad_first
    for n in range(low_ctx):
        input_part = input_part + dot_nn(grad_near[n], qkv_weights[n])
    with jax.named_scope("share_grad_tokens"):
        grad_tokens = place_rows(tp_pieces(turned_rows(input_part)))
    with jax.named_scope("sum_qkv"):
        total = fold_near([dot_tn(g, inputs).astype(BF16) for g in grad_near])
        total = cut(fold_width(fold_half(total)), head_cols)
        pieces = []
        for s in range(tp):
            at = (s // per_group) * 3 * per_group + s % per_group
            pieces.append(jnp.concatenate([total[at + i * per_group] for i in range(3)], 0))
        share_qkv = fold_tp(pieces)
    with jax.named_scope("join_qkv"):
        grad_w_qkv = join_ctx(share_qkv).reshape(ctx, 3, head_cols, width_part)
        grad_w_qkv = grad_w_qkv.transpose(1, 3, 0, 2).reshape(3, width_part, ctx * head_cols)

    def tp_order(values, axis):
        moved = [
            lax.dynamic_index_in_dim(values, (at_tp - t) % tp, axis, True) for t in range(tp)
        ]
        return jnp.concatenate(moved, axis)

    small_sums = jnp.stack(
        [
            v.reshape(-1)
            for v in (
                grad_bias_attn,
                grad_gain_first,
                grad_shift_first,
                grad_bias_out,
                grad_gain_second,
                grad_shift_second,
            )
        ]
    )
    in_sums = grad_bias_in.reshape(low_ctx, 2, tp, hidden).transpose(1, 0, 2, 3)
    in_sums = reorder(in_sums.reshape(ctx, tp, hidden), at_ctx, ctx_bits, 0)
    in_sums = tp_order(in_sums.transpose(1, 0, 2), 0).reshape(-1, width)
    qv_sums = jnp.stack([jnp.sum(g, 0, dtype=F32) for g in grad_near])
    qv_sums = qv_sums.reshape(low_ctx, 2, groups, 3, per_group, head_cols)
    qv_sums = qv_sums.transpose(3, 1, 0, 2, 4, 5).reshape(3, ctx, tp, head_cols)
    qv_sums = reorder(jnp.stack([qv_sums[0], qv_sums[2]]), at_ctx, ctx_bits, 1)
    qv_sums = tp_order(qv_sums.transpose(0, 2, 1, 3), 1).reshape(2, width)
    small_sums = jnp.concatenate([reorder_width(small_sums), in_sums, qv_sums], 0)
    with jax.named_scope("sum_small"):
        for axis, size in (("ctx", ctx), ("fsdp", fsdp), ("tp", tp)):
            for bit in range(size.bit_length() - 1):
                small_sums = small_sums + exchange(small_sums, axis, size, 1 << bit)
    width_sums = lax.dynamic_slice_in_dim(small_sums[:6], at_fsdp * width_part, width_part, 1)
    hidden_own = lax.dynamic_index_in_dim(
        small_sums[6:-2].reshape(tp, b_in.shape[0], fsdp, b_in.shape[1]), at_tp, 0, False
    )
    grad_b_in = lax.dynamic_index_in_dim(hidden_own, at_fsdp, 1, False)
    qv_own = lax.dynamic_index_in_dim(
        small_sums[-2:].reshape(2, tp, head_count, fsdp, head_size // fsdp), at_tp, 1, False
    )
    grad_b_qv = lax.dynamic_index_in_dim(qv_own, at_fsdp, 2, False)
    return (
        output,
        grad_tokens,
        grad_w_qkv,
        grad_b_qv,
        grad_w_o,
        width_sums[0],
        width_sums[1],
        width_sums[2],
        grad_w_in,
        grad_b_in,
        grad_w_out,
        width_sums[3],
        width_sums[4],
        width_sums[5],
    )


def solution(mesh):
    in_specs = (
        P("fsdp", "ctx", None),
        P("fsdp", None),
        P(None, "fsdp", "tp"),
        P(None, "tp", "fsdp"),
        P("tp", "fsdp"),
        P("fsdp"),
        P("fsdp"),
        P("fsdp"),
        P("fsdp", "tp"),
        P("tp", "fsdp"),
        P("tp", "fsdp"),
        P("fsdp"),
        P("fsdp"),
        P("fsdp"),
        P("fsdp", "ctx", None),
    )
    out_specs = (
        P("fsdp", "ctx", None),
        P("fsdp", "ctx", None),
        P(None, "fsdp", "tp"),
        P(None, "tp", "fsdp"),
        P("tp", "fsdp"),
        P("fsdp"),
        P("fsdp"),
        P("fsdp"),
        P("fsdp", "tp"),
        P("tp", "fsdp"),
        P("tp", "fsdp"),
        P("fsdp"),
        P("fsdp"),
        P("fsdp"),
    )
    sizes = tuple(mesh.shape[a] for a in ("fsdp", "ctx", "tp"))
    body = functools.partial(local, sizes)
    return jax.shard_map(body, mesh=mesh, in_specs=in_specs, out_specs=out_specs, check_vma=False)
```

```python
import functools
import itertools
import math

import jax
import jax.numpy as jnp
from jax import lax
from jax.experimental import pallas as pl
from jax.experimental.pallas import tpu as pltpu
from jax.sharding import PartitionSpec as P

EPSILON = 1e-12
NEG_LARGE = -1e30
SCALE_QK = 0.125
LOG2_E = 1.4426950408889634
SCALE_LOG2 = SCALE_QK * LOG2_E
LANES = 128
BF16 = jnp.bfloat16
F32 = jnp.float32
CONTRACT_LAST = (((1,), (1,)), ((), ()))
CONTRACT_FIRST = (((0,), (0,)), ((), ()))


def layer_norm(values, gain_vec, offset):
    center = values - jnp.mean(values, -1, keepdims=True)
    spread = jnp.mean(center * center, -1, keepdims=True)
    return center * lax.rsqrt(spread + EPSILON) * gain_vec + offset


def gelu_exact(values):
    return 0.5 * values * (1.0 + lax.erf(values * 0.7071067811865476))


def gelu_slope(values):
    normal_cdf = 0.5 * (1.0 + lax.erf(values * 0.7071067811865476))
    return normal_cdf + values * jnp.exp(-0.5 * values * values) * 0.3989422804014327


def dot_nt(left, right):
    return lax.dot_general(left, right, CONTRACT_LAST, preferred_element_type=F32)


def dot_tn(left, right):
    return lax.dot_general(left, right, CONTRACT_FIRST, preferred_element_type=F32)


def dot_nn(left, right):
    return jnp.dot(left, right, preferred_element_type=F32)


def assemble(arrays, plan, shapes, name):
    def kernel(*refs):
        ins, outs = refs[: len(arrays)], refs[len(arrays) :]
        for out, row, col, count, wide, sources in plan:
            step = math.gcd(count, 64)

            def body(i, carry, out=out, row=row, col=col, wide=wide, sources=sources, step=step):
                offset = i * step
                parts = []
                for source, at_row, at_col in sources:
                    start = pl.multiple_of(at_row + offset, 16)
                    parts.append(ins[source][pl.ds(start, step), at_col : at_col + wide])
                value = parts[0]
                if len(parts) > 1:
                    value = sum(p.astype(F32) for p in parts).astype(BF16)
                outs[out][pl.ds(pl.multiple_of(row + offset, 16), step), col : col + wide] = value
                return carry

            lax.fori_loop(0, count // step, body, 0)

    size = sum(a.size for a in arrays) + sum(r * c for r, c in shapes)
    return pl.pallas_call(
        kernel,
        in_specs=[pl.BlockSpec(memory_space=pltpu.VMEM)] * len(arrays),
        out_specs=[pl.BlockSpec(memory_space=pltpu.VMEM)] * len(shapes),
        out_shape=[jax.ShapeDtypeStruct(shape, BF16) for shape in shapes],
        cost_estimate=pl.CostEstimate(flops=size, bytes_accessed=2 * size, transcendentals=0),
        name=name,
    )(*arrays)


def attend_kernel(head_size, count, *refs):
    blocks, (sq_ref, sk_ref) = refs[:count], refs[count : count + 2]
    out_refs, lse_ref, qkv = refs[count + 2 : 2 * count + 2], refs[-2], refs[-1]
    step = pl.program_id(1)
    block_len, block = blocks[0].shape[1], sq_ref.shape[1]
    per = block_len // block

    @pl.when(step == 0)
    def _():
        for j in range(count):
            qkv[j * block_len : (j + 1) * block_len, :] = blocks[j][0]

    lane_head = lax.broadcasted_iota(jnp.int32, (1, LANES), 1) // head_size
    query = qkv[pl.ds(pl.multiple_of(step * block, block), block), :LANES]
    key, value = qkv[:, LANES : 2 * LANES], qkv[:, 2 * LANES :]
    same_doc = sq_ref[0] == sk_ref[0]
    heads = LANES // head_size
    mixed = jnp.zeros(query.shape, F32)
    lse = jnp.zeros(query.shape, F32)
    for head in range(heads):
        own = lane_head == head
        scores = dot_nt(jnp.where(own, query, jnp.zeros_like(query)), key)
        scores = jnp.where(same_doc, scores, NEG_LARGE)
        row_max = jnp.max(scores, -1, keepdims=True)
        exp_scores = jnp.exp2((scores - row_max) * SCALE_LOG2)
        denominator = jnp.sum(exp_scores, -1, keepdims=True)
        part = dot_nn(exp_scores.astype(BF16), value) / denominator
        mixed = jnp.where(own, part, mixed)
        lse = jnp.where(own, row_max * SCALE_LOG2 + jnp.log2(denominator), lse)
    mixed = mixed.astype(BF16)
    for j in range(count):

        @pl.when(step // per == j)
        def _(j=j):
            start = pl.multiple_of(step % per * block, block)
            out_refs[j][0, pl.ds(start, block), :] = mixed

    turned = lse.T
    for head in range(heads):
        lse_ref[0, head : head + 1, :] = turned[head * head_size : head * head_size + 1, :]


def attend(blocks, segs, head_size):
    count = len(blocks)
    seq_count, block_len, cols = blocks[0].shape
    length = count * block_len
    block = min(256, block_len)
    elements = seq_count * length * length * LANES
    block_spec = pl.BlockSpec((1, block_len, cols), lambda s, i: (s, 0, 0))
    out_spec = pl.BlockSpec((1, block_len, LANES), lambda s, i: (s, 0, 0))
    results = pl.pallas_call(
        functools.partial(attend_kernel, head_size, count),
        grid=(seq_count, length // block),
        in_specs=[block_spec] * count
        + [
            pl.BlockSpec((1, block, 1), lambda s, i: (s, i, 0)),
            pl.BlockSpec((1, 1, length), lambda s, i: (s, 0, 0)),
        ],
        out_specs=[out_spec] * count + [pl.BlockSpec((1, 8, block), lambda s, i: (s, 0, i))],
        out_shape=[jax.ShapeDtypeStruct((seq_count, block_len, LANES), BF16)] * count
        + [jax.ShapeDtypeStruct((seq_count, 8, length), F32)],
        scratch_shapes=[pltpu.VMEM((length, cols), BF16)],
        compiler_params=pltpu.CompilerParams(vmem_limit_bytes=48 << 20),
        cost_estimate=pl.CostEstimate(
            flops=4 * elements,
            bytes_accessed=8 * seq_count * length * LANES,
            transcendentals=elements // head_size,
        ),
        name="attend",
    )(*blocks, segs[:, :, None], segs[:, None, :])
    return results[:count], results[count]


def attend_grad_kernel(head_size, count, *refs):
    blocks, do_refs, o_refs = refs[:count], refs[count : 2 * count], refs[2 * count : 3 * count]
    sq_ref, sk_ref, lse_ref = refs[3 * count : 3 * count + 3]
    out_refs = refs[3 * count + 3 : 4 * count + 3]
    qkv, grad_seq, mixed_seq, kt_ref, dk_sum, dv_sum = refs[4 * count + 3 :]
    step = pl.program_id(1)
    block_len, block = blocks[0].shape[1], sq_ref.shape[2]
    per = block_len // block

    @pl.when(step == 0)
    def _():
        for j in range(count):
            rows = slice(j * block_len, (j + 1) * block_len)
            qkv[rows, :] = blocks[j][0]
            grad_seq[rows, :] = do_refs[j][0]
            mixed_seq[rows, :] = o_refs[j][0]
        kt_ref[...] = qkv[:, LANES : 2 * LANES].T
        dk_sum[...] = jnp.zeros_like(dk_sum)
        dv_sum[...] = jnp.zeros_like(dv_sum)

    lane_head = lax.broadcasted_iota(jnp.int32, (1, LANES), 1) // head_size
    own_rows = pl.ds(pl.multiple_of(step * block, block), block)
    query, key, value = qkv[own_rows, :LANES], qkv[:, LANES : 2 * LANES], qkv[:, 2 * LANES :]
    grad_out = grad_seq[own_rows, :]
    same_doc = sk_ref[0] == sq_ref[0]
    products = (grad_out.astype(F32) * mixed_seq[own_rows, :].astype(F32)).T
    grad_query = []
    for head in range(LANES // head_size):
        own = lane_head == head
        rows = slice(head * head_size, (head + 1) * head_size)
        row_delta = jnp.sum(products[rows], 0, keepdims=True)
        query_own = jnp.where(own, query, jnp.zeros_like(query))
        grad_own = jnp.where(own, grad_out, jnp.zeros_like(grad_out))
        scores = dot_nt(key, query_own) * SCALE_LOG2 - lse_ref[0, head : head + 1, :]
        probs = jnp.exp2(jnp.where(same_doc, scores, NEG_LARGE))
        grad_probs = dot_nt(value, grad_own)
        grad_scores = (probs * (grad_probs - row_delta)).astype(BF16)
        dv_sum[...] += dot_nn(probs.astype(BF16), grad_own)
        dk_sum[...] += dot_nn(grad_scores, query_own)
        grad_query.append(dot_nn(kt_ref[rows, :], grad_scores))
    grad_query = (jnp.concatenate(grad_query, 0).T * SCALE_QK).astype(BF16)
    for j in range(count):

        @pl.when(step // per == j)
        def _(j=j):
            start = pl.multiple_of(step % per * block, block)
            out_refs[j][0, pl.ds(start, block), :LANES] = grad_query

    @pl.when(step == pl.num_programs(1) - 1)
    def _():
        for j in range(count):
            rows = slice(j * block_len, (j + 1) * block_len)
            out_refs[j][0, :, LANES : 2 * LANES] = (dk_sum[rows, :] * SCALE_QK).astype(BF16)
            out_refs[j][0, :, 2 * LANES :] = dv_sum[rows, :].astype(BF16)


def attend_grad(blocks, grad_blocks, group, mixed_blocks, segs, lse, head_size):
    count = len(blocks)
    seq_count, block_len, cols = blocks[0].shape
    length = count * block_len
    block = min(256, block_len)
    elements = seq_count * length * length * LANES
    block_spec = pl.BlockSpec((1, block_len, cols), lambda s, i: (s, 0, 0))
    return pl.pallas_call(
        functools.partial(attend_grad_kernel, head_size, count),
        grid=(seq_count, length // block),
        in_specs=[block_spec] * count
        + [pl.BlockSpec((1, block_len, LANES), lambda s, i: (s, 0, group))] * count
        + [pl.BlockSpec((1, block_len, LANES), lambda s, i: (s, 0, 0))] * count
        + [
            pl.BlockSpec((1, 1, block), lambda s, i: (s, 0, i)),
            pl.BlockSpec((1, length, 1), lambda s, i: (s, 0, 0)),
            pl.BlockSpec((1, 8, block), lambda s, i: (s, 0, i)),
        ],
        out_specs=[block_spec] * count,
        out_shape=[jax.ShapeDtypeStruct(blocks[0].shape, BF16)] * count,
        scratch_shapes=[
            pltpu.VMEM((length, cols), BF16),
            pltpu.VMEM((length, LANES), BF16),
            pltpu.VMEM((length, LANES), BF16),
            pltpu.VMEM((LANES, length), BF16),
            pltpu.VMEM((length, LANES), F32),
            pltpu.VMEM((length, LANES), F32),
        ],
        compiler_params=pltpu.CompilerParams(vmem_limit_bytes=56 << 20),
        cost_estimate=pl.CostEstimate(
            flops=10 * elements,
            bytes_accessed=16 * seq_count * length * LANES,
            transcendentals=elements // head_size,
        ),
        name="attend_grad",
    )(*blocks, *grad_blocks, *mixed_blocks, segs[:, None, :], segs[:, :, None], lse)


def local(
    sizes,
    tokens,
    segments,
    w_qkv,
    b_qv,
    w_o,
    b_o,
    ln1_gain,
    ln1_bias,
    w_in,
    b_in,
    w_out,
    b_out,
    ln2_gain,
    ln2_bias,
    cotangent,
):
    fsdp, ctx, tp = sizes
    at_fsdp, at_ctx, at_tp = (lax.axis_index(a) for a in ("fsdp", "ctx", "tp"))
    fsdp_bits, ctx_bits = fsdp.bit_length() - 1, ctx.bit_length() - 1
    low_ctx = ctx // 2
    seqs, block_len, width = tokens.shape
    own_seqs = seqs // tp
    rows = own_seqs * block_len
    length = segments.shape[1]
    head_size = b_qv.shape[2] * fsdp
    head_cols = w_qkv.shape[2] // ctx
    hidden = w_in.shape[1] // ctx
    width_part = width // fsdp

    def exchange(values, axis, size, j):
        return lax.ppermute(values, axis, [(i, i ^ j) for i in range(size)])

    def shift_tp(values):
        return lax.ppermute(values, "tp", [(i, (i + 1) % tp) for i in range(tp)])

    def reorder(blocks, place, bits, axis):
        size = blocks.shape[axis]
        for bit in range(bits):
            order = [i ^ (1 << bit) for i in range(size)]
            turned = jnp.stack([lax.index_in_dim(blocks, i, axis, False) for i in order], axis)
            blocks = jnp.where((place >> bit) & 1 == 1, turned, blocks)
        return blocks

    def reorder_width(values):
        for bit in range(fsdp_bits):
            order = [i ^ (1 << bit) for i in range(fsdp)]
            parts = [values[:, i * width_part : (i + 1) * width_part] for i in order]
            values = jnp.where((at_fsdp >> bit) & 1 == 1, jnp.concatenate(parts, 1), values)
        return values

    def tp_pieces(piece):
        pieces = [piece]
        for _ in range(tp - 1):
            piece = shift_tp(piece)
            pieces.append(piece)
        return pieces

    def spread_near(values):
        blocks = [values]
        for bit in range(ctx_bits - 1):
            blocks = blocks + [exchange(b, "ctx", ctx, 1 << bit) for b in blocks]
        return blocks

    def near_rows(values, count, both):
        halves = range(2) if both else range(1)
        return [
            lax.dynamic_slice_in_dim(values, (at_ctx ^ (h * low_ctx)) * count, count, 0)
            for h in halves
        ]

    def cut(values, count):
        return [values[i : i + count] for i in range(0, values.shape[0], count)]

    per_group = max(1, LANES // head_cols)
    groups = tp // per_group
    group_cols = per_group * head_cols
    qkv_turned, w_in_turned = jnp.swapaxes(w_qkv, 1, 2), w_in.T
    qkv_pieces = []
    for h in range(2):
        start = (at_ctx ^ (h * low_ctx)) * head_cols
        qkv_pieces.append(
            lax.dynamic_slice_in_dim(qkv_turned, start, head_cols, 1).reshape(
                3 * head_cols, width_part
            )
        )
    small_width = [v.reshape(1, -1) for v in (b_o, ln1_gain, ln1_bias, b_out, ln2_gain, ln2_bias)]
    small_tail = jnp.concatenate([b_qv.reshape(-1), b_in.reshape(-1)])
    tail_rows = -(-small_tail.shape[0] // width_part)
    small_tail = jnp.pad(small_tail, (0, tail_rows * width_part - small_tail.shape[0]))
    small = jnp.concatenate(small_width + [small_tail.reshape(tail_rows, width_part)], 0)
    small = jnp.pad(small, ((0, -small.shape[0] % 16), (0, 0)))
    small_rows = small.shape[0]
    def gate(values, waited):
        return lax.optimization_barrier((values, waited))

    def width_parts(piece):
        parts = [piece]
        for bit in range(fsdp_bits):
            parts = parts + [exchange(p, "fsdp", fsdp, 1 << bit) for p in parts]
        return parts

    def full_pieces(piece, waits=()):
        pieces = []
        for s in range(tp - 1):
            parts, moved = width_parts(piece), shift_tp(piece)
            (parts, piece), _ = gate((parts, moved), list(waits[s : s + 1]))
            pieces.append(parts)
        return pieces + [width_parts(piece)]

    def place_pieces(pieces, runs, shapes, name):
        arrays = [part for parts in pieces for part in parts]
        plan = [
            (out, row, i * width_part, count, width_part, [(s * fsdp + i, at_row, 0)])
            for out, row, s, at_row, count in runs
            for i in range(fsdp)
        ]
        return assemble(arrays, plan, shapes, name)

    with jax.named_scope("get_qkv"):
        first_pieces = full_pieces(jnp.concatenate(qkv_pieces + [small], 0))
        runs, row = [], 0
        for h, g, i, s in itertools.product(range(2), range(groups), range(3), range(per_group)):
            runs.append((0, row, g * per_group + s, (h * 3 + i) * head_cols, head_cols))
            row += head_cols
        for s in range(tp):
            runs.append((1, s * small_rows, s, 6 * head_cols, small_rows))
        own_qkv, small_full = place_pieces(
            first_pieces, runs, [(row, width), (tp * small_rows, width)], "place_qkv"
        )
        qkv_weights = spread_near(own_qkv)
    small_full = small_full.reshape(tp, small_rows, fsdp, width_part)
    own_small = small_full[0].astype(F32)
    bias_attn, gain_one, shift_one, bias_out, gain_two, shift_two = (
        own_small[i].reshape(1, width) for i in range(6)
    )
    fsdp_order = at_fsdp ^ jnp.arange(fsdp)
    ctx_order = at_ctx ^ jnp.arange(ctx)
    tails = small_full[:, 6 : 6 + tail_rows].astype(F32)
    tails = reorder(tails.transpose(2, 0, 1, 3), at_fsdp, fsdp_bits, 0)
    tails = tails.reshape(fsdp, tp, tail_rows * width_part)
    head_count = b_qv.shape[1]
    qv_tail = tails[:, :, : b_qv.size].reshape(fsdp, tp, 2, head_count, head_size // fsdp)
    qv_bias = qv_tail.transpose(2, 1, 3, 0, 4).reshape(2, tp, ctx, head_cols)
    qv_bias = reorder(qv_bias, at_ctx, ctx_bits, 2)
    in_tail = tails[:, :, b_qv.size : b_qv.size + b_in.size]
    in_tail = in_tail.reshape(fsdp, tp, b_in.shape[0], b_in.shape[1])
    in_bias = in_tail.transpose(1, 2, 0, 3).reshape(tp, ctx, hidden)
    in_bias = reorder(in_bias, at_ctx, ctx_bits, 1).reshape(tp, 2, low_ctx, hidden)
    in_bias = in_bias.transpose(2, 1, 0, 3).reshape(low_ctx, 1, 2 * tp * hidden)
    qv_bias = qv_bias.reshape(2, groups, per_group, 2, low_ctx, head_cols)
    qv_bias = qv_bias.transpose(4, 3, 1, 0, 2, 5).reshape(low_ctx, 2, groups, 2, group_cols)
    qkv_bias = jnp.stack([qv_bias[:, :, :, 0], jnp.zeros_like(qv_bias[:, :, :, 0]), qv_bias[:, :, :, 1]], 3)
    qkv_bias = qkv_bias.reshape(low_ctx, 1, 6 * tp * head_cols)

    def own_rows(values):
        values = lax.dynamic_slice_in_dim(values, at_tp * own_seqs, own_seqs, 0)
        return reorder_width(values.reshape(rows, width))

    inputs, grad_final = own_rows(tokens), own_rows(cotangent)
    own_segments = lax.dynamic_slice_in_dim(segments, at_tp * own_seqs, own_seqs, 0)
    seg_blocks = own_segments.reshape(own_seqs, ctx, block_len)
    segs = jnp.concatenate(
        [lax.dynamic_index_in_dim(seg_blocks, at_ctx ^ j, 1, False) for j in range(ctx)], 1
    )

    aligned = head_cols % head_size == 0
    split_cols = width // ctx
    if not aligned:
        want = ctx_order[:, None] * split_cols + jnp.arange(split_cols)[None, :]
        shard, inner = want // (ctx * head_cols), want % (ctx * head_cols)
        part, offset = inner // head_cols, inner % head_cols
        to_heads = ((part ^ at_ctx) * tp + (at_tp - shard) % tp) * head_cols + offset
        to_heads = to_heads.reshape(-1)
        from_heads = jnp.zeros_like(to_heads).at[to_heads].set(jnp.arange(width))

    def move_columns(blocks, order):
        if aligned:
            return blocks
        parts = blocks[0][0].shape[1] // group_cols
        moved = []
        for i in range(parts):
            cols = slice(i * group_cols, (i + 1) * group_cols)
            flat = jnp.concatenate([b[:, cols] for per in blocks for b in per], 1)
            moved.append(jnp.take(flat, order, axis=1))
        result = []
        for j in range(ctx):
            result.append([])
            for g in range(groups):
                start = j * split_cols + g * group_cols
                result[j].append(
                    jnp.concatenate([m[:, start : start + group_cols] for m in moved], 1)
                )
        return result

    def trade(blocks):
        return [blocks[0]] + [exchange(blocks[j], "ctx", ctx, j) for j in range(1, ctx)]

    def to_sequences(blocks):
        return [b.reshape(own_seqs, block_len, b.shape[1]) for b in trade(blocks)]

    def to_rows(blocks):
        return trade([b.reshape(rows, b.shape[2]) for b in blocks])

    def by_block(near_values, cols):
        return [
            [
                near_values[j % low_ctx][
                    :, ((j // low_ctx) * groups + g) * cols : ((j // low_ctx) * groups + g + 1) * cols
                ]
                for g in range(groups)
            ]
            for j in range(ctx)
        ]

    def by_near(blocks):
        return [
            jnp.concatenate(
                [blocks[h * low_ctx + n][g] for h in range(2) for g in range(groups)], 1
            )
            for n in range(low_ctx)
        ]

    qkv_near = [
        (dot_nt(inputs, qkv_weights[n]) + qkv_bias[n]).astype(BF16) for n in range(low_ctx)
    ]
    qkv_blocks = move_columns(by_block(qkv_near, 3 * group_cols), None if aligned else to_heads)
    heads_in, mixed_parts, mixed_blocks = [], [], [[] for _ in range(ctx)]
    with jax.named_scope("to_sequences"):
        all_seq = [to_sequences([b[g] for b in qkv_blocks]) for g in range(groups)]
    for g in range(groups):
        qkv_seq = all_seq[g]
        mixed, lse = attend(qkv_seq, segs, head_size)
        heads_in.append((qkv_seq, lse))
        mixed_parts.append(mixed)
        with jax.named_scope("to_rows"):
            for j, block in enumerate(to_rows(mixed)):
                mixed_blocks[j].append(block)
    waited = [first_pieces[-1][0]] + [parts[1:] for parts in first_pieces[:-1]]
    waits = [qkv_near, all_seq[0], (all_seq[-1], mixed_parts[0])]
    with jax.named_scope("get_in"):
        piece = jnp.concatenate(
            near_rows(w_o, head_cols, True) + near_rows(w_in_turned, hidden, True), 0
        )
        piece, _ = gate(piece, waited)
        in_pieces = full_pieces(piece, waits)

    def both_halves(pieces, parts, name):
        runs, row, start = [], 0, 0
        for count in parts:
            for h, s in itertools.product(range(2), range(tp)):
                runs.append((0, row, s, start + h * count, count))
                row += count
            start += 2 * count
        return spread_near(place_pieces(pieces, runs, [(row, width)], name)[0])

    with jax.named_scope("get_in"):
        both_weights = both_halves(in_pieces, (head_cols, hidden), "place_in")
        o_rows = 2 * tp * head_cols
        o_weights = [w[:o_rows] for w in both_weights]
        in_weights = [w[o_rows:] for w in both_weights]
    attended = by_near(move_columns(mixed_blocks, None if aligned else from_heads))

    attn_rows = bias_attn
    for n in range(low_ctx):
        attn_rows = attn_rows + dot_nn(attended[n], o_weights[n])
    with jax.named_scope("get_out"):
        piece = jnp.concatenate(near_rows(w_out, hidden, True), 0)
        waited = [in_pieces[-1][0], mixed_parts[0]] + [parts[1:] for parts in in_pieces[:-1]]
        piece, _ = gate(piece, (waited, all_seq[-1]))
        early = [b[0] for b in mixed_blocks[1:]] if groups > 1 else []
        late = [b[-1] for b in mixed_blocks[1:]]
        out_pieces = full_pieces(piece, [(mixed_parts[-1], early), late, attn_rows])
        out_weights = both_halves(out_pieces, (hidden,), "place_out")
    first_in = inputs.astype(F32) + attn_rows
    normed, pull_first = jax.vjp(layer_norm, first_in, gain_one, shift_one)
    normed_low = normed.astype(BF16)
    pre_act = [dot_nt(normed_low, in_weights[n]) + in_bias[n] for n in range(low_ctx)]
    act_low = [gelu_exact(p).astype(BF16) for p in pre_act]
    mlp_rows = bias_out
    for n in range(low_ctx):
        mlp_rows = mlp_rows + dot_nn(act_low[n], out_weights[n])
    final_rows, pull_second = jax.vjp(layer_norm, normed + mlp_rows, gain_two, shift_two)

    def turned_rows(values):
        return reorder_width(values.astype(BF16)).reshape(own_seqs, block_len, width)

    def place_rows(pieces):
        whole = jnp.zeros((seqs, block_len, width), BF16)
        for s in range(tp):
            start = ((at_tp - s) % tp) * own_seqs
            whole = lax.dynamic_update_slice_in_dim(whole, pieces[s], start, 0)
        return whole

    output_pieces = [turned_rows(final_rows)]

    def next_output():
        with jax.named_scope("share_output"):
            return shift_tp(output_pieces[-1]) if len(output_pieces) < tp else output_pieces[0]

    def keep_output(piece):
        if len(output_pieces) < tp:
            output_pieces.append(piece)

    def add_low(left, right):
        return (left.astype(F32) + right.astype(F32)).astype(BF16)

    def fold_width(values, bits=fsdp_bits):
        for bit in reversed(range(bits)):
            half = values.shape[1] // 2
            values = add_low(values[:, :half], exchange(values[:, half:], "fsdp", fsdp, 1 << bit))
        return values

    def fold_half(values):
        half = values.shape[0] // 2
        return add_low(values[:half], exchange(values[half:], "ctx", ctx, low_ctx))

    def fold_tp(pieces):
        total = pieces[0].astype(F32)
        for s in range(1, tp):
            pairs = [(t, (t - s) % tp) for t in range(tp)]
            total = total + lax.ppermute(pieces[s], "tp", pairs).astype(F32)
        return total.astype(BF16)

    def fold_near(near_values):
        for bit in reversed(range(ctx_bits - 1)):
            half = len(near_values) // 2
            near_values = [
                add_low(near_values[n], exchange(near_values[n + half], "ctx", ctx, 1 << bit))
                for n in range(half)
            ]
        return near_values[0]

    def join_ctx(share):
        blocks = share
        for bit in range(ctx_bits):
            blocks = jnp.concatenate([blocks, exchange(blocks, "ctx", ctx, 1 << bit)], 0)
        blocks = blocks.reshape((ctx,) + share.shape)
        return reorder(blocks, at_ctx, ctx_bits, 0).astype(F32)

    grad_second, grad_gain_second, grad_shift_second = pull_second(grad_final.astype(F32))
    grad_mlp = grad_second.astype(BF16)
    grad_bias_out = jnp.sum(grad_mlp, 0, dtype=F32)
    with jax.named_scope("sum_out"):
        sum_out = fold_near([dot_tn(a, grad_mlp).astype(BF16) for a in act_low])
    grad_pre = [
        (dot_nt(grad_mlp, out_weights[n]) * gelu_slope(pre_act[n])).astype(BF16)
        for n in range(low_ctx)
    ]
    grad_pre, (sum_out, piece) = gate(grad_pre, (sum_out, next_output()))
    keep_output(piece)
    with jax.named_scope("sum_out"):
        sum_out = fold_width(sum_out)
    grad_bias_in = jnp.stack([jnp.sum(g, 0, dtype=F32) for g in grad_pre])
    with jax.named_scope("sum_in"):
        grad_in = [dot_tn(g, normed_low).astype(BF16) for g in grad_pre]
    grad_normed = grad_second
    for n in range(low_ctx):
        grad_normed = grad_normed + dot_nn(grad_pre[n], in_weights[n])
    grad_first, grad_gain_first, grad_shift_first = pull_first(grad_normed)
    grad_attn = grad_first.astype(BF16)
    grad_bias_attn = jnp.sum(grad_attn, 0, dtype=F32)
    grad_attended = [dot_nt(grad_attn, o_weights[n]).astype(BF16) for n in range(low_ctx)]
    grad_blocks = move_columns(by_block(grad_attended, group_cols), None if aligned else to_heads)
    with jax.named_scope("to_sequences_grad"):
        grad_mixed = to_sequences([jnp.concatenate(b, 1) for b in grad_blocks])
    with jax.named_scope("sum_in"):
        grad_o = [dot_tn(a, grad_attn).astype(BF16) for a in attended]
        arrays = []
        for near_values in (grad_in, grad_o):
            for bit in reversed(range(1, ctx_bits - 1)):
                half = len(near_values) // 2
                near_values = [
                    add_low(near_values[n], exchange(near_values[n + half], "ctx", ctx, 1 << bit))
                    for n in range(half)
                ]
            arrays.append(near_values[0])
            if ctx_bits > 1:
                arrays.append(exchange(near_values[1], "ctx", ctx, 1))
        each = len(arrays) // 2
        in_half, o_half = tp * hidden, tp * head_cols
        plan, side = [], width // 2
        for h, c in itertools.product(range(2), range(2)):
            row = h * (in_half + o_half)
            for first, at, count in ((0, row, in_half), (each, row + in_half, o_half)):
                sources = [(first + i, h * count, c * side) for i in range(each)]
                plan.append((c, at, 0, count, side, sources))
        sum_in = assemble(arrays, plan, [(2 * (in_half + o_half), side)] * 2, "merge_in")
    grad_mixed, (sum_out, sum_in, piece) = gate(grad_mixed, (sum_out, sum_in, next_output()))
    keep_output(piece)
    with jax.named_scope("sum_in"):
        top = fsdp_bits - 1
        sum_in = add_low(sum_in[0], exchange(sum_in[1], "fsdp", fsdp, 1 << top))
        sum_in = fold_width(sum_in, top)
    with jax.named_scope("sum_out"):
        sum_out = fold_half(sum_out)

    grad_qkv = [[] for _ in range(ctx)]
    for g in range(groups):
        parts, lse = heads_in[g]
        if g == groups - 1:
            parts, (sum_out, piece) = gate(parts, (sum_out, next_output()))
            keep_output(piece)
            with jax.named_scope("sum_out"):
                share_out = fold_tp(cut(sum_out, hidden))
        grads = attend_grad(parts, grad_mixed, g, mixed_parts[g], segs, lse, head_size)
        with jax.named_scope("to_rows_grad"):
            for j, block in enumerate(to_rows(grads)):
                grad_qkv[j].append(block)
    while len(output_pieces) < tp:
        output_pieces.append(next_output())
    output = place_rows(output_pieces)
    grad_qkv, (share_out, sum_in) = gate(grad_qkv, (share_out, sum_in))
    with jax.named_scope("sum_in"):
        sum_in = fold_half(sum_in)
    grad_near = by_near(move_columns(grad_qkv, None if aligned else from_heads))
    input_part = grad_first
    for n in range(low_ctx):
        input_part = input_part + dot_nn(grad_near[n], qkv_weights[n])
    with jax.named_scope("share_grad_tokens"):
        grad_tokens = place_rows(tp_pieces(turned_rows(input_part)))
    def tp_order(values, axis):
        moved = [
            lax.dynamic_index_in_dim(values, (at_tp - t) % tp, axis, True) for t in range(tp)
        ]
        return jnp.concatenate(moved, axis)

    small_sums = jnp.stack(
        [
            v.reshape(-1)
            for v in (
                grad_bias_attn,
                grad_gain_first,
                grad_shift_first,
                grad_bias_out,
                grad_gain_second,
                grad_shift_second,
            )
        ]
    )
    in_sums = grad_bias_in.reshape(low_ctx, 2, tp, hidden).transpose(1, 0, 2, 3)
    in_sums = reorder(in_sums.reshape(ctx, tp, hidden), at_ctx, ctx_bits, 0)
    in_sums = tp_order(in_sums.transpose(1, 0, 2), 0).reshape(-1, width)
    qv_sums = jnp.stack([jnp.sum(g, 0, dtype=F32) for g in grad_near])
    qv_sums = qv_sums.reshape(low_ctx, 2, groups, 3, per_group, head_cols)
    qv_sums = qv_sums.transpose(3, 1, 0, 2, 4, 5).reshape(3, ctx, tp, head_cols)
    qv_sums = reorder(jnp.stack([qv_sums[0], qv_sums[2]]), at_ctx, ctx_bits, 1)
    qv_sums = tp_order(qv_sums.transpose(0, 2, 1, 3), 1).reshape(2, width)
    small_sums = jnp.concatenate([reorder_width(small_sums), in_sums, qv_sums], 0)

    def sum_small(values, axis, size, bits):
        with jax.named_scope("sum_small"):
            for bit in bits:
                values = values + exchange(values, axis, size, 1 << bit)
        return values

    with jax.named_scope("sum_qkv"):
        total = fold_near([dot_tn(g, inputs).astype(BF16) for g in grad_near])
        small_sums = sum_small(small_sums, "ctx", ctx, range(ctx_bits - 1))
        (total, small_sums), _ = gate((total, small_sums), ())
        total = fold_half(total)
        small_sums = sum_small(small_sums, "ctx", ctx, range(ctx_bits - 1, ctx_bits))
        (total, small_sums, sum_in), _ = gate((total, small_sums, sum_in), ())
        total = fold_width(total)
    with jax.named_scope("sum_in"):
        in_rows = tp * hidden
        in_cut, o_cut = cut(sum_in[:in_rows], hidden), cut(sum_in[in_rows:], head_cols)
        share_in = fold_tp([jnp.concatenate([i, o], 0) for i, o in zip(in_cut, o_cut)])
    with jax.named_scope("sum_qkv"):
        (total, share_in, small_sums), _ = gate((total, share_in, small_sums), ())
        small_sums = sum_small(small_sums, "fsdp", fsdp, range(fsdp_bits))
        total = cut(total, head_cols)
        pieces = []
        for s in range(tp):
            at = (s // per_group) * 3 * per_group + s % per_group
            pieces.append(jnp.concatenate([total[at + i * per_group] for i in range(3)], 0))
        share_qkv = fold_tp(pieces)
    with jax.named_scope("join_out_in"):
        joined = join_ctx(jnp.concatenate([share_out, share_in], 0))
        grad_w_out = joined[:, :hidden].reshape(ctx * hidden, width_part)
        grad_w_in = joined[:, hidden : 2 * hidden].reshape(ctx * hidden, width_part).T
        grad_w_o = joined[:, 2 * hidden :].reshape(ctx * head_cols, width_part)
    with jax.named_scope("join_qkv"):
        (share_qkv, small_sums), _ = gate((share_qkv, small_sums), ())
        grad_w_qkv = join_ctx(share_qkv).reshape(ctx, 3, head_cols, width_part)
        grad_w_qkv = grad_w_qkv.transpose(1, 3, 0, 2).reshape(3, width_part, ctx * head_cols)
        small_sums = sum_small(small_sums, "tp", tp, range(tp.bit_length() - 1))
    width_sums = lax.dynamic_slice_in_dim(small_sums[:6], at_fsdp * width_part, width_part, 1)
    hidden_own = lax.dynamic_index_in_dim(
        small_sums[6:-2].reshape(tp, b_in.shape[0], fsdp, b_in.shape[1]), at_tp, 0, False
    )
    grad_b_in = lax.dynamic_index_in_dim(hidden_own, at_fsdp, 1, False)
    qv_own = lax.dynamic_index_in_dim(
        small_sums[-2:].reshape(2, tp, head_count, fsdp, head_size // fsdp), at_tp, 1, False
    )
    grad_b_qv = lax.dynamic_index_in_dim(qv_own, at_fsdp, 2, False)
    return (
        output,
        grad_tokens,
        grad_w_qkv,
        grad_b_qv,
        grad_w_o,
        width_sums[0],
        width_sums[1],
        width_sums[2],
        grad_w_in,
        grad_b_in,
        grad_w_out,
        width_sums[3],
        width_sums[4],
        width_sums[5],
    )


def solution(mesh):
    in_specs = (
        P("fsdp", "ctx", None),
        P("fsdp", None),
        P(None, "fsdp", "tp"),
        P(None, "tp", "fsdp"),
        P("tp", "fsdp"),
        P("fsdp"),
        P("fsdp"),
        P("fsdp"),
        P("fsdp", "tp"),
        P("tp", "fsdp"),
        P("tp", "fsdp"),
        P("fsdp"),
        P("fsdp"),
        P("fsdp"),
        P("fsdp", "ctx", None),
    )
    out_specs = (
        P("fsdp", "ctx", None),
        P("fsdp", "ctx", None),
        P(None, "fsdp", "tp"),
        P(None, "tp", "fsdp"),
        P("tp", "fsdp"),
        P("fsdp"),
        P("fsdp"),
        P("fsdp"),
        P("fsdp", "tp"),
        P("tp", "fsdp"),
        P("tp", "fsdp"),
        P("fsdp"),
        P("fsdp"),
        P("fsdp"),
    )
    sizes = tuple(mesh.shape[a] for a in ("fsdp", "ctx", "tp"))
    body = functools.partial(local, sizes)
    return jax.shard_map(body, mesh=mesh, in_specs=in_specs, out_specs=out_specs, check_vma=False)
```
